32 devices in a mesh: dp: 4 (over z), ctx: 4 (over y, core), tensor: 2 (over x).
Axes of the slice: x: 2, y: 2, z: 4, core: 2. Of those that a mesh axis runs over, the one named last changes fastest.
Arguments:
- tokens: bfloat16 [8192, 4, 1280], P(('ctx', 'tensor'), 'dp'), may hold values from -6 to 6
- segments: int32 [4, 8192], P('dp'), may hold values from 0 to 31, never falling along the last dimension, each value on 1 to 4096 neighbouring positions
- gain_attn: float32 [1280], replicated, may hold values from 0.5 to 1.5
- query_scale: float32 [80], replicated, may hold values from -3 to 3
- w_qkv: bfloat16 [3, 1280, 1280], P(None, ('dp', 'ctx'), 'tensor'), may hold values from -0.15625 to 0.15625
- w_out: bfloat16 [1280, 1280], P('tensor', ('dp', 'ctx')), may hold values from -1 to 1
- gain_mlp: float32 [1280], replicated, may hold values from 0.5 to 1.5
- w_up: bfloat16 [1280, 1280], P(('dp', 'ctx'), 'tensor'), may hold values from -0.15625 to 0.15625
- b_up: float32 [1280], replicated, may hold values from -3 to 3
- w_down: bfloat16 [1280, 1280], P('tensor', ('dp', 'ctx')), may hold values from -0.15625 to 0.15625
- b_down: float32 [1280], replicated, may hold values from -3 to 3
- cotangent: bfloat16 [8192, 4, 1280], P(('ctx', 'tensor'), 'dp'), may hold values from -6 to 6
Outputs:
- outputs: bfloat16 [8192, 4, 1280], P(('ctx', 'tensor'), 'dp')
- grad_inputs: bfloat16 [8192, 4, 1280], P(('ctx', 'tensor'), 'dp')
- grad_w_qkv: float32 [3, 1280, 1280], P(None, ('dp', 'ctx'), 'tensor')
- grad_w_out: float32 [1280, 1280], P('tensor', ('dp', 'ctx'))
- grad_w_up: float32 [1280, 1280], P(('dp', 'ctx'), 'tensor')
- grad_w_down: float32 [1280, 1280], P('tensor', ('dp', 'ctx'))
- grad_gain_attn: float32 [1280], replicated
- grad_query_scale: float32 [80], replicated
- grad_gain_mlp: float32 [1280], replicated
- grad_b_up: float32 [1280], replicated
- grad_b_down: float32 [1280], replicated
The draws below stay inside these ranges and needn't reach their ends.
Inputs may be any that keep to these rules, and one draw needn't show every extreme that they name: `segments`: along each sequence the ids never fall; a document is a run of equal ids of at most 4096 positions.
All inputs are finite; a program needn't handle non-finite values.
Results may differ from the reference program's by a relative error of at most 0.018.
Values may be sent and summed in bfloat16 or wider, within the bound.
No kernel may reach another device: no remote copies, remote signals or barrier semaphores. Data moves between devices by JAX's collectives and lax.ppermute only.
A program may use at most 768 MiB of HBM per device.

```python
import math
import jax
import jax.numpy as jnp
import numpy as np
from jax import lax

D = 1280
HEADS = 16
HD = 80
H = 1280
LEN = 8192
QB = 512
SEQS = 4


def block_scale(key, extent, pieces, least, high):
    def one(dim, blocks):
        heights = jax.random.uniform(jax.random.fold_in(jax.random.fold_in(key, 6), dim), (blocks,), jnp.float32, least / len(pieces), high / len(pieces))
        return jnp.repeat(jnp.exp(heights), extent[dim] // blocks).reshape((-1,) + (1,) * (len(extent) - dim - 1))

    factor_of = one(*pieces[0])
    for cut in pieces[1:]:
        factor_of = factor_of * one(*cut)
    return factor_of


def profile(amount, total, limit, lean):
    portions = [(1 << 20) // math.isqrt(standing ** lean) + 1 for standing in range(2, amount + 1)]
    rest, holding = total - limit - (amount - 1), [1] * (amount - 1)
    while rest > 0:
        candidates = [i for i in range(amount - 1) if holding[i] < limit]
        whole, remaining = sum([portions[i] for i in candidates]), rest
        for i in candidates:
            extra = min(limit - holding[i], max(1, remaining * portions[i] // whole), rest)
            holding[i] = holding[i] + extra
            rest = rest - extra
    return np.array([limit] + holding)


def uneven(stream_key, count, total, bound, skew):
    if count == 2:
        one = jax.random.randint(stream_key, (), max(1, total - bound), min(bound, total - 1) + 1)
        return jnp.stack([one, total - one])
    tallies = jnp.asarray(profile(count, total, bound, skew), jnp.int32)
    twos = (count - 1) // 2
    source_of, taker = tallies[1:1 + 2 * twos:2], tallies[2:2 + 2 * twos:2]
    room = jnp.minimum(source_of - 1, bound - taker)
    passed = jax.random.randint(jax.random.fold_in(stream_key, 1), (twos,), 0, 1 << 20) % (room + 1)
    tallies = tallies.at[1:1 + 2 * twos:2].set(source_of - passed).at[2:2 + 2 * twos:2].set(taker + passed)
    return tallies[jax.random.permutation(jax.random.fold_in(stream_key, 2), count)]


def normal_values(rng, extent, width, most, pieces=(), kind=jnp.bfloat16):
    level = block_scale(rng, extent, pieces, -0.22, 0.18) if pieces else 1.0
    array = jax.random.normal(rng, extent, jnp.float32) * width * level
    return jnp.minimum(jnp.maximum(array, -most), most).astype(kind)


def setup_inputs(seed: int = 0) -> dict:
    key_list = jax.random.split(jax.random.key(seed), 13)
    return {
        "tokens": normal_values(key_list[0], (LEN, SEQS, D), 1.0, 6.0, ((0, 8), (1, 4))),
        "segments": jax.vmap(lambda own: jnp.searchsorted(jnp.cumsum(uneven(own, max(4, LEN // 256), LEN, LEN // 2, 2)), jnp.arange(LEN), side="right"))(jax.random.split(key_list[1], SEQS)).reshape((SEQS, LEN)).astype(jnp.int32),
        "gain_attn": jnp.clip(1.0 + 0.1 * jax.random.normal(key_list[2], (D,), jnp.float32), 0.5, 1.5),
        "query_scale": normal_values(key_list[3], (HD,), 0.5, 3.0, (), jnp.float32),
        "w_qkv": normal_values(key_list[4], (3, D, D), D ** -0.5, 0.15625, ((1, 16), (2, 2))),
        "w_out": normal_values(key_list[5], (D, D), (D // 32) ** -0.5, 1.0, ((0, 2), (1, 16))),
        "gain_mlp": jnp.clip(1.0 + 0.1 * jax.random.normal(key_list[6], (D,), jnp.float32), 0.5, 1.5),
        "w_up": normal_values(key_list[7], (D, H), D ** -0.5, 0.15625, ((0, 16), (1, 2))),
        "b_up": normal_values(key_list[8], (H,), 0.5, 3.0, (), jnp.float32),
        "w_down": normal_values(key_list[9], (H, D), H ** -0.5, 0.15625, ((0, 2), (1, 16))),
        "b_down": normal_values(key_list[10], (D,), 0.5, 3.0, (), jnp.float32),
        "cotangent": normal_values(key_list[11], (LEN, SEQS, D), 1.0, 6.0, ((0, 8), (1, 4))),
    }


@jax.custom_vjp
def low(v):
    return lax.optimization_barrier(v.astype(jnp.bfloat16)).astype(jnp.float32)

@jax.custom_vjp
def low_back(v):
    return v

def low_keep(v):
    return (low(v), None)

def low_pass(kept, grad):
    return (grad,)

def back_keep(v):
    return (v, None)

def back_low(kept, grad):
    return (low(grad),)
low.defvjp(low_keep, low_pass)
low_back.defvjp(back_keep, back_low)
EPSILON = 1e-06
LOG_TWO_E = 1.442695041
NEGATIVE = -1e+30
HIGH = lax.Precision.HIGHEST

def rms_norm(values, gain):
    return values * lax.rsqrt(lax.optimization_barrier(jnp.mean(values * values, axis=-1, keepdims=True)) + EPSILON) * gain

def attend_sequence(queries, keys, values, seg_ids):
    key_pos = jnp.arange(LEN, dtype=jnp.int32)

    def one_block(number):
        first = number * QB
        q_block = lax.dynamic_slice_in_dim(queries, first, QB, 0)
        seg_query = lax.dynamic_slice_in_dim(seg_ids, first, QB, 0)
        query_pos = first + jnp.arange(QB, dtype=jnp.int32)
        raw_scores = low_back(jnp.einsum('qhe,khe->hqk', q_block, keys, precision=HIGH))
        allowed = (key_pos[None, :] <= query_pos[:, None]) & (seg_ids[None, :] == seg_query[:, None])
        masked = jnp.where(allowed[None], raw_scores, NEGATIVE)
        probs = jax.nn.softmax(masked, axis=-1)
        return jnp.einsum('hqk,khe->qhe', low(probs), values, precision=HIGH)
    blocks = lax.map(jax.checkpoint(one_block), jnp.arange(LEN // QB, dtype=jnp.int32))
    return blocks.reshape(LEN, HEADS, HD)

def layer(segments, inputs, gain_attn, query_scale, w_qkv, w_out, gain_mlp, w_up, b_up, w_down, b_down):
    normed_one = low(rms_norm(inputs, gain_attn))
    projected = jnp.einsum('lsd,cde->clse', normed_one, w_qkv, precision=HIGH)
    scaling = LOG_TWO_E / math.sqrt(HD) * jax.nn.softplus(query_scale)
    shaped = projected.reshape(3, LEN, SEQS, HEADS, HD)
    queries = low(low_back(shaped[0]) * scaling)
    keys = low(low_back(shaped[1]))
    values = low(low_back(shaped[2]))
    heads_out = lax.map(lambda item: attend_sequence(item[0], item[1], item[2], item[3]), (queries.transpose(1, 0, 2, 3), keys.transpose(1, 0, 2, 3), values.transpose(1, 0, 2, 3), segments))
    mixed = low(low_back(heads_out.transpose(1, 0, 2, 3).reshape(LEN, SEQS, D)))
    attended = low_back(jnp.einsum('lse,ed->lsd', mixed, w_out, precision=HIGH))
    hidden = inputs + attended
    normed_two = low(rms_norm(hidden, gain_mlp))
    pre_act = low_back(jnp.einsum('lsd,dh->lsh', normed_two, w_up, precision=HIGH) + b_up)
    activation = low(jax.nn.silu(pre_act))
    return hidden + (jnp.einsum('lsh,hd->lsd', activation, w_down, precision=HIGH) + b_down)

def reference(tokens, segments, gain_attn, query_scale, w_qkv, w_out, gain_mlp, w_up, b_up, w_down, b_down, cotangent):
    floats = [value.astype(jnp.float32) for value in (tokens, gain_attn, query_scale, w_qkv, w_out, gain_mlp, w_up, b_up, w_down, b_down)]
    outputs, pull = jax.vjp(lambda *values: layer(segments, *values), *floats)
    grads = pull(cotangent.astype(jnp.float32))
    return (outputs.astype(jnp.bfloat16), grads[0].astype(jnp.bfloat16), grads[3], grads[4], grads[6], grads[8], grads[1], grads[2], grads[5], grads[7], grads[9])
```

```python
import functools
import math

import jax
import jax.numpy as jnp
from jax import lax
from jax.experimental import pallas as pl
from jax.experimental.layout import Layout, with_layout_constraint
from jax.experimental.pallas import tpu as pltpu
from jax.sharding import PartitionSpec as P

HD = 80
IDS = 32
BLOCK_Q = 512
BLOCK_K = 512
EPSILON = 1e-06
LOG_TWO_E = 1.442695041
LOG2E = 1.4426950408889634
NEGATIVE = -1e30
VMEM_BYTES = 60 << 20
bf16, f32 = jnp.bfloat16, jnp.float32


def dot(a, b, contract_a, contract_b):
    return lax.dot_general(
        a, b, ((contract_a, contract_b), ((), ())), preferred_element_type=f32
    )


def nn(a, b):
    return dot(a, b, (1,), (0,))


def nt(a, b):
    return dot(a, b, (1,), (1,))


def attend_body(lo_ref, clean_ref, x_ref, start_ref, o_ref, wide_ref, lse_ref, key_rows, *, chunks, chunk):
    per_q, per_k = chunk // BLOCK_Q, chunk // BLOCK_K
    for c in range(chunks):
        key_rows[pl.ds(c * chunk, chunk), :] = x_ref[c, 0, 1].T

    def query_block(i, _):
        c = i // per_q
        off = pl.multiple_of((i % per_q) * BLOCK_Q, BLOCK_Q)
        q = x_ref[c, 0, 0, :, pl.ds(off, BLOCK_Q)]
        first = start_ref[0, pl.ds(c, 1), pl.ds(off, BLOCK_Q)]
        query_pos = i * BLOCK_Q + lax.broadcasted_iota(jnp.int32, (BLOCK_K, BLOCK_Q), 1)
        key_iota = lax.broadcasted_iota(jnp.int32, (BLOCK_K, BLOCK_Q), 0)

        def step(masked, j, carry):
            top, total, acc = carry
            k = key_rows[pl.ds(pl.multiple_of(j * BLOCK_K, BLOCK_K), BLOCK_K), :]
            scores = nn(k, q) * LOG2E
            if masked:
                key_pos = j * BLOCK_K + key_iota
                scores = jnp.where((key_pos <= query_pos) & (key_pos >= first), scores, NEGATIVE)
            new_top = jnp.maximum(top, jnp.max(scores, axis=0, keepdims=True))
            weights = jnp.exp2(scores - new_top)
            shrink = jnp.exp2(top - new_top)
            total = total * shrink + jnp.sum(weights, axis=0, keepdims=True)
            v = x_ref[j // per_k, 0, 2, :, pl.ds(pl.multiple_of((j % per_k) * BLOCK_K, BLOCK_K), BLOCK_K)]
            acc = acc * shrink + nn(v, weights.astype(bf16))
            return new_top, total, acc

        carry = (
            jnp.full((1, BLOCK_Q), NEGATIVE, f32),
            jnp.zeros((1, BLOCK_Q), f32),
            jnp.zeros((HD, BLOCK_Q), f32),
        )
        diagonal = (i * BLOCK_Q) // BLOCK_K
        end = (i * BLOCK_Q + BLOCK_Q - 1) // BLOCK_K + 1
        carry = lax.fori_loop(diagonal, end, functools.partial(step, True), carry)
        carry = lax.fori_loop(clean_ref[i], diagonal, functools.partial(step, False), carry)
        carry = lax.fori_loop(lo_ref[i], clean_ref[i], functools.partial(step, True), carry)
        top, total, acc = carry
        result = acc / total
        o_ref[c, :, pl.ds(off, BLOCK_Q)] = result.astype(bf16)
        wide_ref[c, :, pl.ds(off, BLOCK_Q)] = result
        lse_ref[0, pl.ds(c, 1), pl.ds(off, BLOCK_Q)] = top + jnp.log2(total)
        return 0

    lax.fori_loop(0, chunks * per_q, query_block, 0)


def attend_back_body(
    hi_ref, clean_ref, x_ref, g_ref, wide_ref, lse_ref, start_ref, scale_ref,
    dx_ref, part_ref, dq, dk, dv, delta, *, chunks, chunk,
):
    per_q, per_k = chunk // BLOCK_Q, chunk // BLOCK_K
    for c in range(chunks):
        delta[c : c + 1, :] = jnp.sum(g_ref[c].astype(f32) * wide_ref[c], axis=0, keepdims=True)
        dq[c] = jnp.zeros((HD, chunk), f32)

    def key_block(j, _):
        cj = j // per_k
        koff = pl.multiple_of((j % per_k) * BLOCK_K, BLOCK_K)
        kt = x_ref[cj, 0, 1, :, pl.ds(koff, BLOCK_K)]
        k = kt.T
        v = x_ref[cj, 0, 2, :, pl.ds(koff, BLOCK_K)].T
        dk[...] = jnp.zeros_like(dk)
        dv[...] = jnp.zeros_like(dv)
        key_pos = j * BLOCK_K + lax.broadcasted_iota(jnp.int32, (BLOCK_K, BLOCK_Q), 0)
        query_iota = lax.broadcasted_iota(jnp.int32, (BLOCK_K, BLOCK_Q), 1)

        def step(masked, i, _):
            c = i // per_q
            off = pl.multiple_of((i % per_q) * BLOCK_Q, BLOCK_Q)
            q = x_ref[c, 0, 0, :, pl.ds(off, BLOCK_Q)]
            g = g_ref[c, :, pl.ds(off, BLOCK_Q)]
            scores = nn(k, q) * LOG2E
            if masked:
                first = start_ref[0, pl.ds(c, 1), pl.ds(off, BLOCK_Q)]
                query_pos = i * BLOCK_Q + query_iota
                scores = jnp.where((key_pos <= query_pos) & (key_pos >= first), scores, NEGATIVE)
            probs = jnp.exp2(scores - lse_ref[0, pl.ds(c, 1), pl.ds(off, BLOCK_Q)])
            grad_raw = probs * (nn(v, g) - delta[pl.ds(c, 1), pl.ds(off, BLOCK_Q)])
            low = grad_raw.astype(bf16)
            dv[...] += nt(g, probs.astype(bf16))
            dk[...] += nt(q, low)
            dq[c, :, pl.ds(off, BLOCK_Q)] += nn(kt, low)
            return 0

        diagonal = (j * BLOCK_K) // BLOCK_Q
        end = (j * BLOCK_K + BLOCK_K - 1) // BLOCK_Q + 1
        lax.fori_loop(diagonal, end, functools.partial(step, True), 0)
        lax.fori_loop(end, clean_ref[j], functools.partial(step, False), 0)
        lax.fori_loop(clean_ref[j], hi_ref[j], functools.partial(step, True), 0)
        dx_ref[cj, 1, :, pl.ds(koff, BLOCK_K)] = dk[...].astype(bf16)
        dx_ref[cj, 2, :, pl.ds(koff, BLOCK_K)] = dv[...].astype(bf16)
        return 0

    lax.fori_loop(0, chunks * per_k, key_block, 0)
    part = jnp.zeros((HD, 128), f32)
    for c in range(chunks):
        grad = dq[c]
        dx_ref[c, 0] = (grad * scale_ref[:, 0:1]).astype(bf16)
        term = grad * x_ref[c, 0, 0].astype(f32)
        for u in range(chunk // 128):
            part = part + term[:, u * 128 : (u + 1) * 128]
    part_ref[...] = part


def kernel_cost(length, matmuls):
    pairs = length * 2048
    return pl.CostEstimate(
        flops=matmuls * 512 * pairs, bytes_accessed=length * 2048, transcendentals=pairs
    )


def attend(tables, x, start, p):
    chunks, _, _, _, chunk = x.shape
    flat = lambda g, *_: (0, 0, 0)
    return pl.pallas_call(
        functools.partial(attend_body, chunks=chunks, chunk=chunk),
        grid_spec=pltpu.PrefetchScalarGridSpec(
            num_scalar_prefetch=2,
            grid=(1,),
            in_specs=[
                pl.BlockSpec((chunks, 1, 3, HD, chunk), lambda g, *_: (0, p, 0, 0, 0)),
                pl.BlockSpec((1, chunks, chunk), flat),
            ],
            out_specs=[
                pl.BlockSpec((chunks, HD, chunk), flat),
                pl.BlockSpec((chunks, HD, chunk), flat),
                pl.BlockSpec((1, chunks, chunk), flat),
            ],
            scratch_shapes=[pltpu.VMEM((chunks * chunk, HD), bf16)],
        ),
        out_shape=[
            jax.ShapeDtypeStruct((chunks, HD, chunk), bf16),
            jax.ShapeDtypeStruct((chunks, HD, chunk), f32),
            jax.ShapeDtypeStruct((1, chunks, chunk), f32),
        ],
        compiler_params=pltpu.CompilerParams(vmem_limit_bytes=VMEM_BYTES),
        cost_estimate=kernel_cost(chunks * chunk, 2),
        name="attend",
    )(*tables, x, start)


def attend_back(tables, x, grad, wide, lse, start, scale, p):
    chunks, _, _, _, chunk = x.shape
    flat = lambda g, *_: (0, 0, 0)
    return pl.pallas_call(
        functools.partial(attend_back_body, chunks=chunks, chunk=chunk),
        grid_spec=pltpu.PrefetchScalarGridSpec(
            num_scalar_prefetch=2,
            grid=(1,),
            in_specs=[
                pl.BlockSpec((chunks, 1, 3, HD, chunk), lambda g, *_: (0, p, 0, 0, 0)),
                pl.BlockSpec((chunks, HD, chunk), flat),
                pl.BlockSpec((chunks, HD, chunk), flat),
                pl.BlockSpec((1, chunks, chunk), flat),
                pl.BlockSpec((1, chunks, chunk), flat),
                pl.BlockSpec((HD, 128), lambda g, *_: (0, 0)),
            ],
            out_specs=[
                pl.BlockSpec((chunks, 3, HD, chunk), lambda g, *_: (0, 0, 0, 0)),
                pl.BlockSpec((HD, 128), lambda g, *_: (0, 0)),
            ],
            scratch_shapes=[
                pltpu.VMEM((chunks, HD, chunk), f32),
                pltpu.VMEM((HD, BLOCK_K), f32),
                pltpu.VMEM((HD, BLOCK_K), f32),
                pltpu.VMEM((chunks, chunk), f32),
            ],
        ),
        out_shape=[
            jax.ShapeDtypeStruct((chunks, 3, HD, chunk), bf16),
            jax.ShapeDtypeStruct((HD, 128), f32),
        ],
        compiler_params=pltpu.CompilerParams(vmem_limit_bytes=VMEM_BYTES),
        cost_estimate=kernel_cost(chunks * chunk, 5),
        name="attend_back",
    )(*tables, x, grad, wide, lse, start, scale)


def weight_grad_body(me_ref, *refs, spots):
    n = len(spots)
    pieces, (w_ref, *dxs), (out_ref, gain_ref), (buffers, acc, lhs, sems) = (
        refs[:n], refs[n:-6], refs[-6:-4], refs[-4:]
    )
    features = 3 * HD

    def copy(i):
        rows = spots[i][2]
        return pltpu.make_async_copy(pieces[i], buffers.at[i % 2, pl.ds(0, rows)], sems.at[i % 2])

    copy(0).start()
    for i, (distance, first, rows) in enumerate(spots):
        if i + 1 < n:
            copy(i + 1).start()
        chunk = me_ref[0] ^ distance
        for p, dx in enumerate(dxs):
            for c in range(3):
                lhs[p * features + c * HD : p * features + (c + 1) * HD, 0:rows] = dx[
                    chunk, c, :, first : first + rows
                ]
        copy(i).wait()
        width = acc.shape[1]
        for lane in range(0, width, 256):
            part = nn(lhs[:, 0:rows], buffers[i % 2, 0:rows, lane : lane + 256])
            if i:
                part = part + acc[:, lane : lane + 256]
            acc[:, lane : lane + 256] = part
    total = acc[...]
    out_ref[...] = total.astype(bf16)
    gain_ref[...] = jnp.sum(total * w_ref[...].astype(f32), axis=0, keepdims=True)


def weight_grad(me, pieces, spots, w_rows, dxs):
    features, width = w_rows.shape
    rows = max(n for _, _, n in spots)
    whole = pl.BlockSpec(memory_space=pltpu.VMEM)
    return pl.pallas_call(
        functools.partial(weight_grad_body, spots=spots),
        in_specs=[pl.BlockSpec(memory_space=pltpu.SMEM)]
        + [pl.BlockSpec(memory_space=pl.ANY)] * len(pieces)
        + [whole] * (1 + len(dxs)),
        out_specs=[whole, whole],
        out_shape=[
            jax.ShapeDtypeStruct((features, width), bf16),
            jax.ShapeDtypeStruct((1, width), f32),
        ],
        scratch_shapes=[
            pltpu.VMEM((2, rows, width), bf16),
            pltpu.VMEM((features, width), f32),
            pltpu.VMEM((features, rows), bf16),
            pltpu.SemaphoreType.DMA((2,)),
        ],
        compiler_params=pltpu.CompilerParams(vmem_limit_bytes=VMEM_BYTES),
        cost_estimate=pl.CostEstimate(
            flops=2 * features * width * sum(n for _, _, n in spots),
            bytes_accessed=2 * width * sum(n for _, _, n in spots),
            transcendentals=0,
        ),
        name="weight_grad",
    )(me, *pieces, w_rows, *dxs)


def block_tables(segments):
    length = segments.shape[0]
    ids = jnp.arange(IDS, dtype=jnp.int32)
    below = jnp.sum(segments[None, :] < ids[:, None], axis=1, dtype=jnp.int32)
    upto = jnp.sum(segments[None, :] <= ids[:, None], axis=1, dtype=jnp.int32)
    hot = segments[None, :] == ids[:, None]
    start = jnp.sum(jnp.where(hot, below[:, None], 0), axis=0)
    end = jnp.sum(jnp.where(hot, upto[:, None], 0), axis=0) - 1
    q_block = jnp.arange(length // BLOCK_Q, dtype=jnp.int32)
    k_block = jnp.arange(length // BLOCK_K, dtype=jnp.int32)
    start_first, start_last = start[::BLOCK_Q], start[BLOCK_Q - 1 :: BLOCK_Q]
    lo = start_first // BLOCK_K
    clean = (start_last + BLOCK_K - 1) // BLOCK_K
    clean = jnp.maximum(jnp.minimum(clean, q_block * BLOCK_Q // BLOCK_K), lo)
    end_first, end_last = end[::BLOCK_K], end[BLOCK_K - 1 :: BLOCK_K]
    after = (k_block * BLOCK_K + BLOCK_K - 1) // BLOCK_Q + 1
    hi = end_last // BLOCK_Q + 1
    q_clean = jnp.minimum(jnp.maximum((end_first + 1) // BLOCK_Q, after), hi)
    return start, (lo, clean), (hi, q_clean)


def in_rows(grad):
    return with_layout_constraint(grad.astype(bf16), Layout((0, 1)))


def inverse_rms(values):
    return lax.rsqrt(jnp.mean(values * values, axis=-1, keepdims=True) + EPSILON)


def norm_back(grad_norm, unit, inverse, gain):
    grad_unit = grad_norm * gain
    return inverse * (grad_unit - unit * jnp.mean(grad_unit * unit, axis=-1, keepdims=True))


def per_device(
    tokens,
    segments,
    gain_attn,
    query_scale,
    w_qkv,
    w_out,
    gain_mlp,
    w_up,
    b_up,
    w_down,
    b_down,
    cotangent,
):
    n_dp, n_ctx, n_tensor = (lax.axis_size(a) for a in ("dp", "ctx", "tensor"))
    ctx_rank, tensor_rank = lax.axis_index("ctx"), lax.axis_index("tensor")
    rows, sequences, width = tokens.shape
    shard, columns = w_qkv.shape[1:]
    local_heads = columns // HD
    group = n_ctx * n_tensor
    length = rows * group
    data = ("dp", "ctx")
    everyone = ("dp", "ctx", "tensor")
    split = local_heads % n_ctx == 0
    ctx_parts = n_ctx if split else 1
    own = local_heads // ctx_parts
    owners = ("ctx", "tensor") if split else ("tensor",)
    n_owners = ctx_parts * n_tensor
    head_width = own * 3 * HD

    inputs = tokens[:, 0].astype(f32)
    inverse_one = inverse_rms(inputs)
    unit_one = inputs * inverse_one
    normed_one = (unit_one * gain_attn).astype(bf16)

    def tensor_pair(x):
        if n_tensor != 2:
            return lax.all_gather(x, "tensor", axis=0)
        other = lax.ppermute(x, "tensor", [(0, 1), (1, 0)])
        first = tensor_rank == 0
        return jnp.stack([jnp.where(first, x, other), jnp.where(first, other, x)])

    def scatter_pair(x):
        if n_tensor != 2:
            return lax.psum_scatter(x, "tensor", scatter_dimension=0, tiled=False).astype(f32)
        keep = jnp.where(tensor_rank == 0, x[0], x[1])
        send = jnp.where(tensor_rank == 0, x[1], x[0])
        return keep.astype(f32) + lax.ppermute(send, "tensor", [(0, 1), (1, 0)]).astype(f32)

    def by_distance(x, rank):
        count = x.shape[0]
        bit = 1
        while bit < count:
            y = x.reshape((count // (2 * bit), 2, bit) + x.shape[1:])
            y = jnp.where((rank & bit) > 0, jnp.flip(y, 1), y)
            x = y.reshape(x.shape)
            bit *= 2
        return x

    def exchange(x, axis, rank):
        count = x.shape[0]
        if count & (count - 1):
            return lax.all_to_all(x, axis, 0, 0)
        x = by_distance(x, rank)
        got = [x[0]] + [
            lax.ppermute(x[k], axis, [(i, i ^ k) for i in range(count)]) for k in range(1, count)
        ]
        return by_distance(jnp.stack(got), rank)

    qkv_rows = w_qkv.reshape(3, shard, ctx_parts, own, HD)
    for_owner = qkv_rows.transpose(2, 1, 3, 0, 4).reshape(ctx_parts, shard, head_width)
    if split:
        for_owner = exchange(for_owner, "ctx", ctx_rank)
        normed_one, for_owner = lax.optimization_barrier((normed_one, for_owner))
        owner_w = lax.all_gather(for_owner, "dp", axis=0).reshape(width, head_width)
    else:
        owner_w = lax.all_gather(for_owner[0], data, axis=0).reshape(width, head_width)

    start, forward_tables, backward_tables = block_tables(segments[0])
    qkv_cols = w_qkv.reshape(3, shard, ctx_parts, own, HD).transpose(1, 3, 2, 0, 4)
    out_cols = w_out.T.reshape(shard, ctx_parts, own, HD).transpose(0, 2, 1, 3)
    pair = tensor_pair(
        jnp.concatenate(
            [qkv_cols.reshape(shard, 3 * columns), out_cols.reshape(shard, columns), w_up, w_down.T], axis=1
        )
    )

    def interleave(x, inner):
        x = x.reshape(n_tensor, shard, own * ctx_parts, inner)
        return x.transpose(1, 2, 0, 3).reshape(shard, -1)

    def side_by_side(x):
        return x.transpose(1, 0, 2).reshape(shard, -1)

    full_rows = jnp.stack(
        [
            interleave(pair[..., 3 * columns : 4 * columns], HD),
            side_by_side(pair[..., 4 * columns : 5 * columns]),
            side_by_side(pair[..., 5 * columns :]),
        ]
    )
    qkv_rows_full = interleave(pair[..., : 3 * columns], 3 * HD)
    heads_x = jnp.zeros((group, head_width, rows), bf16)
    scaling = LOG_TWO_E / math.sqrt(HD) * jax.nn.softplus(query_scale)
    scale_rows = jnp.tile(
        jnp.concatenate([scaling, jnp.ones((2 * HD,), f32)]), own
    )[:, None]

    def project(piece):
        return (dot(owner_w, piece, (0,), (1,)) * scale_rows).astype(bf16)

    if group == 8 and n_tensor == 2:
        me = ctx_rank * n_tensor + tensor_rank

        def swap(x, bit):
            return lax.ppermute(x, ("ctx", "tensor"), [(i, i ^ bit) for i in range(group)])

        def add(heads_x, at, piece):
            distance, first, _ = at
            return lax.dynamic_update_slice(heads_x, project(piece)[None], (me ^ distance, 0, first))

        half = rows // 2
        spots = [(0, 0, rows), (2, 0, rows)]
        pieces = [normed_one, swap(normed_one, 2)]
        for at, piece in zip(spots, pieces, strict=True):
            heads_x = add(heads_x, at, piece)
        w_rows = owner_w.T
        (over_x, over_y, heads_x, w_rows, full_rows, qkv_rows_full, start, forward_tables, backward_tables) = (
            lax.optimization_barrier(
                (swap(normed_one, 1), swap(normed_one, 4), heads_x, w_rows, full_rows, qkv_rows_full,
                 start, forward_tables, backward_tables)
            )
        )
        corner_low = swap(over_x[:half], 4)
        corner_high = swap(over_y[half:], 1)
        for at, piece in (
            ((1, 0, rows), over_x),
            ((4, 0, rows), over_y),
            ((5, 0, half), corner_low),
            ((5, half, half), corner_high),
        ):
            for bit in (0, 2):
                spots.append((at[0] ^ bit, *at[1:]))
                pieces.append(swap(piece, 2) if bit else piece)
                heads_x = add(heads_x, spots[-1], pieces[-1])
    else:
        spots = None
        normed_all = lax.all_gather(normed_one, ("ctx", "tensor"), axis=0)
        heads_x = project(normed_all.reshape(length, width)).reshape(head_width, group, rows).transpose(1, 0, 2)

    whole = lax.all_gather(full_rows, data, axis=1, tiled=True)
    out_t, up_all, down_t = whole[0], whole[1], whole[2]
    qkv_all = lax.all_gather(qkv_rows_full, data, axis=0, tiled=True)

    chunk = max(rows, BLOCK_Q, BLOCK_K)
    merge = chunk // rows
    chunks = length // chunk

    def to_chunks(x):
        if merge == 1:
            return x
        x = jnp.moveaxis(x.reshape((chunks, merge) + x.shape[1:]), 1, -2)
        return x.reshape(x.shape[:-2] + (chunk,))

    def from_chunks(x):
        if merge == 1:
            return x
        x = jnp.moveaxis(x.reshape(x.shape[:-1] + (merge, rows)), -2, 1)
        return x.reshape((group,) + x.shape[2:])

    def to_tokens(x):
        x = from_chunks(x)
        if not split:
            x = lax.dynamic_slice_in_dim(x, ctx_rank * n_tensor, n_tensor, 0)
        return lax.all_to_all(x, owners, 0, 0)

    def to_heads(x):
        x = lax.all_to_all(x, owners, 0, 0)
        if not split:
            x = lax.all_gather(x, "ctx", axis=0, tiled=True)
        return to_chunks(x)

    heads_x = to_chunks(heads_x)
    heads_x = heads_x.reshape(chunks, own, 3, HD, chunk)
    start = start.reshape(1, chunks, chunk)

    part = n_owners * HD

    mixed, wides, lses = [], [], []
    for p in range(own):
        o, wide, lse = attend(forward_tables, heads_x, start, p)
        wides.append(wide)
        lses.append(lse)
        mixed.append(to_tokens(o).reshape(part, rows))

    hidden = inputs
    for p in range(own):
        hidden = hidden + dot(mixed[p], out_t[:, p * part : (p + 1) * part], (0,), (1,))
    inverse_two = inverse_rms(hidden)
    unit_two = hidden * inverse_two
    normed_two = (unit_two * gain_mlp).astype(bf16)
    pre_act = nn(normed_two, up_all) + b_up
    sigma = jax.nn.sigmoid(pre_act)
    activation = (pre_act * sigma).astype(bf16)
    outputs = (hidden + (nt(activation, down_t) + b_down)).astype(bf16)

    top_low = cotangent[:, 0]
    grad_top = top_low.astype(f32)
    grad_pre = (nn(top_low, down_t) * (sigma * (1 + pre_act * (1 - sigma)))).astype(bf16)
    grad_normed_two = nt(grad_pre, up_all)
    grad_hidden = grad_top + norm_back(grad_normed_two, unit_two, inverse_two, gain_mlp)
    grad_hidden_low = grad_hidden.astype(bf16)
    grad_heads = [
        to_heads(nt(out_t[:, p * part : (p + 1) * part].T, grad_hidden_low).astype(bf16).reshape(n_owners, HD, rows))
        for p in range(own)
    ]
    grad_out_t = [dot(grad_hidden_low, m, (0,), (1,)) for m in mixed]
    grad_up = dot(normed_two, grad_pre, (0,), (0,))
    grad_down_t = dot(top_low, activation, (0,), (0,))
    stacked = jnp.concatenate([in_rows(g) for g in (*grad_out_t, grad_up, grad_down_t)], axis=1)
    stacked, qkv_all = lax.optimization_barrier((stacked, qkv_all))
    reduced = lax.psum_scatter(stacked, data, scatter_dimension=0, tiled=True)
    reduced = [reduced[:, n * width : (n + 1) * width] for n in range(3)]
    gain_two = jnp.sum(grad_normed_two * unit_two, axis=0)
    bias_up = jnp.sum(grad_pre.astype(f32), axis=0)
    bias_down = jnp.sum(grad_top, axis=0)
    split_out = reduced[0].reshape(shard, own, ctx_parts, n_tensor, HD).transpose(3, 0, 2, 1, 4)
    split_up, split_down = (
        reduced[n].reshape(shard, n_tensor, columns).transpose(1, 0, 2) for n in (1, 2)
    )
    mine = scatter_pair(
        jnp.stack([split_out.reshape(n_tensor, shard, columns), split_up, split_down], axis=1)
    )
    out_grad, up_grad, down_grad = mine[0].T, mine[1], mine[2].T

    scale_tile = jnp.broadcast_to(scaling[:, None], (HD, 128))
    scale_sum = jnp.zeros((HD,), f32)
    gain_part = jnp.zeros((width,), f32)
    dxs, backs = [], []
    for p in range(own):
        if p:
            heads_x, grad_heads[p], dxs[p - 1] = lax.optimization_barrier((heads_x, grad_heads[p], dxs[p - 1]))
        dx, part_sum = attend_back(
            backward_tables, heads_x, grad_heads[p], wides[p], lses[p], start, scale_tile, p
        )
        scale_sum = scale_sum + jnp.sum(part_sum, axis=1)
        if p:
            dx, backs[-1] = lax.optimization_barrier((dx, backs[-1]))
        dxs.append(dx)
        backs.append(to_tokens(dx).reshape(3 * part, rows))
    if spots is None:
        grad_ws = []
        for p in range(own):
            grad_w = lax.dot_general(
                to_chunks(jnp.swapaxes(normed_all, 1, 2)),
                dxs[p].reshape(chunks, 3 * HD, chunk),
                (((0, 2), (0, 2)), ((), ())),
                preferred_element_type=f32,
            )
            weights_p = owner_w.reshape(width, own, 3 * HD)[:, p].astype(f32)
            gain_part = gain_part + jnp.sum(grad_w * weights_p, axis=1)
            grad_ws.append(grad_w.astype(bf16))
        piece = jnp.concatenate(grad_ws, axis=1)
    else:
        piece, gain_part = weight_grad(me.reshape(1), pieces, spots, w_rows, dxs)
        piece, gain_part = piece.T, gain_part[0]
    piece = piece.reshape(n_dp, n_ctx * shard, head_width)
    gain_one, scale_sum = gain_part / gain_attn, scale_sum / scaling
    if not split:
        once = (ctx_rank == 0).astype(f32)
        gain_one, scale_sum = gain_one * once, scale_sum * once
    def back_one(p):
        return dot(backs[p], qkv_all[:, p * 3 * part : (p + 1) * 3 * part], (0,), (1,))

    grad_normed_one = sum((back_one(p) for p in range(own - 1)), jnp.zeros((), f32))
    dp_rank = lax.axis_index("dp")
    sums = jnp.concatenate([gain_one, gain_two, bias_up, bias_down, scale_sum])
    if n_dp == 4 and n_ctx == 4 and n_tensor == 2:

        def across(x, axis, bit):
            return lax.ppermute(x, axis, [(i, i ^ bit) for i in range(lax.axis_size(axis))])

        for bit in (2, 1):
            upper = (dp_rank & bit) > 0
            kept = jnp.where(upper, piece[bit:], piece[:bit])
            sent = jnp.where(upper, piece[:bit], piece[bit:])
            piece = (kept.astype(f32) + across(sent, "dp", bit).astype(f32)).astype(bf16)
            sums = sums + across(sums, "dp", bit)
            piece, sums, out_grad, up_grad, down_grad = lax.optimization_barrier(
                (piece, sums, out_grad, up_grad, down_grad)
            )
        piece = piece[0]
        backs[-1], piece, sums, grad_normed_one = lax.optimization_barrier(
            (backs[-1], piece, sums, grad_normed_one)
        )
        sums = sums + across(sums, "ctx", 1) + across(sums, "ctx", 2) + across(sums, "ctx", 3)
        sums = sums + across(sums, "tensor", 1)
    else:
        piece = jnp.sum(lax.all_to_all(piece, "dp", 0, 0).astype(f32), axis=0).astype(bf16)
        sums = lax.psum(sums, everyone)
    piece = piece.reshape(n_ctx, shard, head_width)
    if split:
        piece = exchange(piece, "ctx", ctx_rank)
    else:
        piece = lax.dynamic_slice_in_dim(piece, ctx_rank, 1, 0)
    qkv_grad = piece.reshape(ctx_parts, shard, own, 3, HD).transpose(3, 1, 0, 2, 4)
    qkv_grad = qkv_grad.reshape(w_qkv.shape).astype(f32)

    grad_normed_one = grad_normed_one + back_one(own - 1)
    grad_inputs = grad_hidden + norm_back(grad_normed_one, unit_one, inverse_one, gain_attn)
    gain_one, gain_two, bias_up, bias_down = (sums[n * width : (n + 1) * width] for n in range(4))
    grad_query_scale = sums[4 * width :] * (LOG_TWO_E / math.sqrt(HD)) * jax.nn.sigmoid(query_scale)
    return (
        outputs[:, None],
        grad_inputs.astype(bf16)[:, None],
        qkv_grad,
        out_grad,
        up_grad,
        down_grad,
        gain_one,
        grad_query_scale,
        gain_two,
        bias_up,
        bias_down,
    )


def solution(mesh):
    placed = (
        P(("ctx", "tensor"), "dp", None),
        P("dp", None),
        P(),
        P(),
        P(None, ("dp", "ctx"), "tensor"),
        P("tensor", ("dp", "ctx")),
        P(),
        P(("dp", "ctx"), "tensor"),
        P(),
        P("tensor", ("dp", "ctx")),
        P(),
        P(("ctx", "tensor"), "dp", None),
    )
    return jax.shard_map(
        per_device,
        mesh=mesh,
        in_specs=placed,
        out_specs=(
            P(("ctx", "tensor"), "dp", None),
            P(("ctx", "tensor"), "dp", None),
            P(None, ("dp", "ctx"), "tensor"),
            P("tensor", ("dp", "ctx")),
            P(("dp", "ctx"), "tensor"),
            P("tensor", ("dp", "ctx")),
            P(),
            P(),
            P(),
            P(),
            P(),
        ),
        check_vma=False,
    )
```

```python
import functools
import math

import jax
import jax.numpy as jnp
from jax import lax
from jax.experimental import pallas as pl
from jax.experimental.layout import Layout, with_layout_constraint
from jax.experimental.pallas import tpu as pltpu
from jax.sharding import PartitionSpec as P

HD = 80
IDS = 32
BLOCK_Q = 512
BLOCK_K = 512
PARTS = 2
WIDE = HD + IDS
EPSILON = 1e-06
LOG_TWO_E = 1.442695041
LOG2E = 1.4426950408889634
NEGATIVE = -1e30
VMEM_BYTES = 60 << 20
bf16, f32 = jnp.bfloat16, jnp.float32


def dot(a, b, contract_a, contract_b):
    return lax.dot_general(
        a, b, ((contract_a, contract_b), ((), ())), preferred_element_type=f32
    )


def nn(a, b):
    return dot(a, b, (1,), (0,))


def nt(a, b):
    return dot(a, b, (1,), (1,))


def place(block, per, size):
    return block // per, pl.multiple_of((block % per) * size, size)


def run_tiles(length, count, tiles, prepare, process):
    n_q, n_k = length // BLOCK_Q, length // BLOCK_K

    def diagonal(t):
        t = jnp.minimum(t, n_q - 1)
        return t * n_k + t * BLOCK_Q // BLOCK_K

    def turns(number, tile, masked):
        prepare(tile(0), 0)

        def turn(t, _):
            prepare(tile(2 * t + 1), 1)
            process(tile(2 * t), 0, masked)
            prepare(tile(2 * t + 2), 0)
            process(tile(2 * t + 1), 1, masked)
            return 0

        lax.fori_loop(0, number, turn, 0)

    turns(n_q // 2, diagonal, True)
    turns(count[0] // 2, lambda t: tiles[t], False)


def attend_body(count, tiles, x_ref, segment_ref, o_ref, wide_ref, lse_ref, key_rows, query_cols, acc, top, total, scores, *, chunks, chunk):
    nk = chunks * chunk // BLOCK_K
    per_q, per_k = chunk // BLOCK_Q, chunk // BLOCK_K
    lanes = BLOCK_Q // PARTS
    for c in range(chunks):
        hot = lax.broadcasted_iota(jnp.int32, (IDS, chunk), 0) == segment_ref[0, c : c + 1, :]
        keys = jnp.concatenate([x_ref[c, 0, 1], jnp.where(hot, 1.0, 0.0).astype(bf16)], axis=0)
        key_rows[pl.ds(c * chunk, chunk), :] = keys.T
        query_cols[c] = jnp.concatenate([x_ref[c, 0, 0], jnp.where(hot, 0.0, NEGATIVE).astype(bf16)], axis=0)
        acc[c] = jnp.zeros((HD, chunk), f32)
    top[...] = jnp.full(top.shape, NEGATIVE, f32)
    total[...] = jnp.zeros(total.shape, f32)
    key_iota = lax.broadcasted_iota(jnp.int32, (BLOCK_K, lanes), 0)
    query_iota = lax.broadcasted_iota(jnp.int32, (BLOCK_K, lanes), 1)

    def prepare(tile, slot):
        c, off = place(tile // nk, per_q, BLOCK_Q)
        k = key_rows[pl.ds(pl.multiple_of((tile % nk) * BLOCK_K, BLOCK_K), BLOCK_K), :]
        for u in range(PARTS):
            scores[slot, :, u * lanes : (u + 1) * lanes] = nn(k, query_cols[c, :, pl.ds(off + u * lanes, lanes)]) * LOG2E

    def process(tile, slot, masked):
        i, j = tile // nk, tile % nk
        c, off = place(i, per_q, BLOCK_Q)
        ck_, koff = place(j, per_k, BLOCK_K)
        v = x_ref[ck_, 0, 2, :, pl.ds(koff, BLOCK_K)]
        for u in range(PARTS):
            at = pl.ds(off + u * lanes, lanes)
            row = pl.ds(c, 1)
            s = scores[slot, :, u * lanes : (u + 1) * lanes]
            if masked:
                s = jnp.where(key_iota - query_iota <= i * BLOCK_Q + u * lanes - j * BLOCK_K, s, NEGATIVE)
            old = top[row, at]
            new = jnp.maximum(old, jnp.max(s, axis=0, keepdims=True))
            p = jnp.exp2(s - new)
            shrink = jnp.exp2(old - new)
            top[row, at] = new
            total[row, at] = total[row, at] * shrink + jnp.sum(p, axis=0, keepdims=True)
            acc[c, :, at] = acc[c, :, at] * shrink + nn(v, p.astype(bf16))

    run_tiles(chunks * chunk, count, tiles, prepare, process)
    for c in range(chunks):
        t = total[c : c + 1, :]
        o = acc[c] / t
        wide_ref[c] = o
        o_ref[c] = o.astype(bf16)
        lse_ref[0, c : c + 1, :] = top[c : c + 1, :] + jnp.log2(t)


def attend_back_body(count, tiles, x_ref, g_ref, wide_ref, lse_ref, segment_ref, scale_ref, dx_ref, part_ref, key_rows, query_cols, value_rows, dq, dk, dv, delta, scores, grads, *, chunks, chunk):
    nk = chunks * chunk // BLOCK_K
    per_q, per_k = chunk // BLOCK_Q, chunk // BLOCK_K
    lanes = BLOCK_Q // PARTS
    for c in range(chunks):
        hot = lax.broadcasted_iota(jnp.int32, (IDS, chunk), 0) == segment_ref[0, c : c + 1, :]
        keys = jnp.concatenate([x_ref[c, 0, 1], jnp.where(hot, 1.0, 0.0).astype(bf16)], axis=0)
        key_rows[pl.ds(c * chunk, chunk), :] = keys.T
        query_cols[c] = jnp.concatenate([x_ref[c, 0, 0], jnp.where(hot, 0.0, NEGATIVE).astype(bf16)], axis=0)
        value_rows[pl.ds(c * chunk, chunk), :] = x_ref[c, 0, 2].T
        delta[c : c + 1, :] = jnp.sum(g_ref[c].astype(f32) * wide_ref[c], axis=0, keepdims=True)
        for ref in (dq, dk, dv):
            ref[c] = jnp.zeros((HD, chunk), f32)
    key_iota = lax.broadcasted_iota(jnp.int32, (BLOCK_K, lanes), 0)
    query_iota = lax.broadcasted_iota(jnp.int32, (BLOCK_K, lanes), 1)

    def prepare(tile, slot):
        c, off = place(tile // nk, per_q, BLOCK_Q)
        rows = pl.ds(pl.multiple_of((tile % nk) * BLOCK_K, BLOCK_K), BLOCK_K)
        k, v = key_rows[rows, :], value_rows[rows, :]
        for u in range(PARTS):
            at = pl.ds(off + u * lanes, lanes)
            scores[slot, :, u * lanes : (u + 1) * lanes] = nn(k, query_cols[c, :, at])
            grads[slot, :, u * lanes : (u + 1) * lanes] = nn(v, g_ref[c, :, at])

    def process(tile, slot, masked):
        i, j = tile // nk, tile % nk
        c, off = place(i, per_q, BLOCK_Q)
        kc, koff = place(j, per_k, BLOCK_K)
        kat = pl.ds(koff, BLOCK_K)
        kt = x_ref[kc, 0, 1, :, kat]
        for u in range(PARTS):
            at = pl.ds(off + u * lanes, lanes)
            row = pl.ds(c, 1)
            s = scores[slot, :, u * lanes : (u + 1) * lanes] * LOG2E
            if masked:
                s = jnp.where(key_iota - query_iota <= i * BLOCK_Q + u * lanes - j * BLOCK_K, s, NEGATIVE)
            p = jnp.exp2(s - lse_ref[0, row, at])
            low = (p * (grads[slot, :, u * lanes : (u + 1) * lanes] - delta[row, at])).astype(bf16)
            q, g = x_ref[c, 0, 0, :, at], g_ref[c, :, at]
            dv[kc, :, kat] += nt(g, p.astype(bf16))
            dk[kc, :, kat] += nt(q, low)
            dq[c, :, at] += nn(kt, low)

    run_tiles(chunks * chunk, count, tiles, prepare, process)
    part = jnp.zeros((HD, 128), f32)
    for c in range(chunks):
        grad = dq[c]
        dx_ref[c, 0] = (grad * scale_ref[:, 0:1]).astype(bf16)
        dx_ref[c, 1] = dk[c].astype(bf16)
        dx_ref[c, 2] = dv[c].astype(bf16)
        term = grad * x_ref[c, 0, 0].astype(f32)
        for u in range(chunk // 128):
            part = part + term[:, u * 128 : (u + 1) * 128]
    part_ref[...] = part


def kernel_cost(length, matmuls):
    pairs = length * 2048
    return pl.CostEstimate(
        flops=matmuls * 512 * pairs, bytes_accessed=length * 2048, transcendentals=pairs
    )


def attend(tables, x, segments, p):
    chunks, _, _, _, chunk = x.shape
    flat = lambda g, *_: (0, 0, 0)
    return pl.pallas_call(
        functools.partial(attend_body, chunks=chunks, chunk=chunk),
        grid_spec=pltpu.PrefetchScalarGridSpec(
            num_scalar_prefetch=2,
            grid=(1,),
            in_specs=[
                pl.BlockSpec((chunks, 1, 3, HD, chunk), lambda g, *_: (0, p, 0, 0, 0)),
                pl.BlockSpec((1, chunks, chunk), flat),
            ],
            out_specs=[
                pl.BlockSpec((chunks, HD, chunk), flat),
                pl.BlockSpec((chunks, HD, chunk), flat),
                pl.BlockSpec((1, chunks, chunk), flat),
            ],
            scratch_shapes=[
                pltpu.VMEM((chunks * chunk, WIDE), bf16),
                pltpu.VMEM((chunks, WIDE, chunk), bf16),
                pltpu.VMEM((chunks, HD, chunk), f32),
                pltpu.VMEM((chunks, chunk), f32),
                pltpu.VMEM((chunks, chunk), f32),
                pltpu.VMEM((2, BLOCK_K, BLOCK_Q), f32),
            ],
        ),
        out_shape=[
            jax.ShapeDtypeStruct((chunks, HD, chunk), bf16),
            jax.ShapeDtypeStruct((chunks, HD, chunk), f32),
            jax.ShapeDtypeStruct((1, chunks, chunk), f32),
        ],
        compiler_params=pltpu.CompilerParams(vmem_limit_bytes=VMEM_BYTES),
        cost_estimate=kernel_cost(chunks * chunk, 2),
        name="attend",
    )(*tables, x, segments)


def attend_back(tables, x, grad, wide, lse, segments, scale, p):
    chunks, _, _, _, chunk = x.shape
    flat = lambda g, *_: (0, 0, 0)
    return pl.pallas_call(
        functools.partial(attend_back_body, chunks=chunks, chunk=chunk),
        grid_spec=pltpu.PrefetchScalarGridSpec(
            num_scalar_prefetch=2,
            grid=(1,),
            in_specs=[
                pl.BlockSpec((chunks, 1, 3, HD, chunk), lambda g, *_: (0, p, 0, 0, 0)),
                pl.BlockSpec((chunks, HD, chunk), flat),
                pl.BlockSpec((chunks, HD, chunk), flat),
                pl.BlockSpec((1, chunks, chunk), flat),
                pl.BlockSpec((1, chunks, chunk), flat),
                pl.BlockSpec((HD, 128), lambda g, *_: (0, 0)),
            ],
            out_specs=[
                pl.BlockSpec((chunks, 3, HD, chunk), lambda g, *_: (0, 0, 0, 0)),
                pl.BlockSpec((HD, 128), lambda g, *_: (0, 0)),
            ],
            scratch_shapes=[
                pltpu.VMEM((chunks * chunk, WIDE), bf16),
                pltpu.VMEM((chunks, WIDE, chunk), bf16),
                pltpu.VMEM((chunks * chunk, HD), bf16),
                pltpu.VMEM((chunks, HD, chunk), f32),
                pltpu.VMEM((chunks, HD, chunk), f32),
                pltpu.VMEM((chunks, HD, chunk), f32),
                pltpu.VMEM((chunks, chunk), f32),
                pltpu.VMEM((2, BLOCK_K, BLOCK_Q), f32),
                pltpu.VMEM((2, BLOCK_K, BLOCK_Q), f32),
            ],
        ),
        out_shape=[
            jax.ShapeDtypeStruct((chunks, 3, HD, chunk), bf16),
            jax.ShapeDtypeStruct((HD, 128), f32),
        ],
        compiler_params=pltpu.CompilerParams(vmem_limit_bytes=VMEM_BYTES),
        cost_estimate=kernel_cost(chunks * chunk, 5),
        name="attend_back",
    )(*tables, x, grad, wide, lse, segments, scale)


def project_body(slots_ref, w_ref, scale_ref, *refs, places):
    n = len(places)
    pieces, (out_ref, done_ref, buffers, results, in_sems, out_sems) = refs[:n], refs[-6:]
    done_ref[...] = jnp.zeros(done_ref.shape, f32)

    def fetch(i):
        return pltpu.make_async_copy(pieces[i], buffers.at[i], in_sems.at[i])

    def store(i):
        first, rows = places[i], results.shape[2]
        return pltpu.make_async_copy(
            results.at[i], out_ref.at[slots_ref[i], :, pl.ds(first, rows)], out_sems.at[i]
        )

    for i in range(n):
        fetch(i).start()
    for i in range(n):
        fetch(i).wait()
        results[i] = (nt(w_ref[...], buffers[i]) * scale_ref[...]).astype(bf16)
        store(i).start()
    for i in range(n):
        store(i).wait()


def project_into(heads, after, shape, slots, places, w, scale, pieces):
    features, width = w.shape
    n, rows = len(pieces), pieces[0].shape[0]
    kept = [] if heads is None else [heads]
    tail = [] if after is None else [after]
    whole = pl.BlockSpec(memory_space=pltpu.VMEM)
    anywhere = pl.BlockSpec(memory_space=pl.ANY)
    return pl.pallas_call(
        functools.partial(project_body, places=places),
        in_specs=[pl.BlockSpec(memory_space=pltpu.SMEM), whole, whole] + [anywhere] * (n + len(kept) + len(tail)),
        out_specs=[anywhere, whole],
        out_shape=[jax.ShapeDtypeStruct(shape, bf16), jax.ShapeDtypeStruct((8, 128), f32)],
        scratch_shapes=[
            pltpu.VMEM((n, rows, width), bf16),
            pltpu.VMEM((n, features, rows), bf16),
            pltpu.SemaphoreType.DMA((n,)),
            pltpu.SemaphoreType.DMA((n,)),
        ],
        input_output_aliases={3 + n: 0} if kept else {},
        compiler_params=pltpu.CompilerParams(vmem_limit_bytes=VMEM_BYTES),
        cost_estimate=pl.CostEstimate(
            flops=2 * n * features * width * rows, bytes_accessed=4 * n * width * rows, transcendentals=0
        ),
        name="project",
    )(slots, w, scale, *pieces, *kept, *tail)


def weight_grad_body(me_ref, *refs, spots):
    n = len(spots)
    pieces, (w_ref, dx, out_ref, gain_ref, buffers, acc, sems) = refs[:n], refs[n:]
    rows, width = buffers.shape[1:]

    def copy(i):
        return pltpu.make_async_copy(pieces[i], buffers.at[i], sems.at[i])

    for i in range(n):
        copy(i).start()
    for i, (distance, first) in enumerate(spots):
        part_dx = dx[me_ref[0] ^ distance, :, :, first : first + rows]
        part_dx = part_dx.reshape(part_dx.shape[0] * part_dx.shape[1], rows)
        copy(i).wait()
        for lane in range(0, width, 256):
            part = nn(part_dx, buffers[i, :, lane : lane + 256])
            acc[:, lane : lane + 256] = part + acc[:, lane : lane + 256] if i else part
    total = acc[...]
    out_ref[...] = total.astype(bf16)
    gain_ref[...] = jnp.sum(total * w_ref[...].astype(f32), axis=0, keepdims=True)


def weight_grad(me, pieces, spots, w, dx):
    features, width = w.shape
    whole = pl.BlockSpec(memory_space=pltpu.VMEM)
    return pl.pallas_call(
        functools.partial(weight_grad_body, spots=spots),
        in_specs=[pl.BlockSpec(memory_space=pltpu.SMEM)]
        + [pl.BlockSpec(memory_space=pl.ANY)] * len(pieces)
        + [whole] * 2,
        out_specs=[whole, whole],
        out_shape=[
            jax.ShapeDtypeStruct((features, width), bf16),
            jax.ShapeDtypeStruct((1, width), f32),
        ],
        scratch_shapes=[
            pltpu.VMEM((len(pieces),) + pieces[0].shape, bf16),
            pltpu.VMEM((features, width), f32),
            pltpu.SemaphoreType.DMA((len(pieces),)),
        ],
        compiler_params=pltpu.CompilerParams(vmem_limit_bytes=VMEM_BYTES),
        cost_estimate=pl.CostEstimate(flops=1, bytes_accessed=1, transcendentals=0),
        name="weight_grad",
    )(me, *pieces, w, dx)


def back_one_body(back_ref, w_ref, out_ref):
    out_ref[...] = nn(w_ref[...], back_ref[...]).T


def finish_body(back_ref, w_ref, other_ref, tokens_ref, gain_ref, hidden_ref, out_ref):
    grad_normed = other_ref[...] + nn(w_ref[...], back_ref[...]).T
    inputs = tokens_ref[...].astype(f32)
    inverse = inverse_rms(inputs)
    out_ref[...] = (
        hidden_ref[...] + norm_back(grad_normed, inputs * inverse, inverse, gain_ref[...])
    ).astype(bf16)


def input_grad(back, w, p, others):
    features, rows = back.shape
    width = w.shape[0]
    block = math.gcd(rows, 256)
    by_tokens = pl.BlockSpec((block, width), lambda t: (t, 0))
    specs = [by_tokens, by_tokens, pl.BlockSpec((1, width), lambda t: (0, 0)), by_tokens] if others else []
    return pl.pallas_call(
        finish_body if others else back_one_body,
        grid=(rows // block,),
        in_specs=[
            pl.BlockSpec((features, block), lambda t: (0, t)),
            pl.BlockSpec((width, features), lambda t: (0, p)),
        ]
        + specs,
        out_specs=by_tokens,
        out_shape=jax.ShapeDtypeStruct((rows, width), bf16 if others else f32),
        compiler_params=pltpu.CompilerParams(vmem_limit_bytes=VMEM_BYTES),
        cost_estimate=pl.CostEstimate(
            flops=2 * features * width * rows if others else 1,
            bytes_accessed=16 * width * rows if others else 1,
            transcendentals=0,
        ),
        name="input_grad",
    )(back, w, *others)


def tile_list(segments):
    length = segments.shape[0]
    n_q, n_k = length // BLOCK_Q, length // BLOCK_K
    first = jnp.sum(segments[None, :] < segments[::BLOCK_Q][:, None], axis=1, dtype=jnp.int32)[:, None]
    q_block = jnp.arange(n_q, dtype=jnp.int32)[:, None]
    k_last = jnp.arange(n_k, dtype=jnp.int32)[None, :] * BLOCK_K + BLOCK_K - 1
    below = ((k_last < q_block * BLOCK_Q) & (k_last >= first)).reshape(-1)
    pair = jnp.arange(n_q * n_k, dtype=jnp.int32)
    rank = jnp.sum(jnp.where((pair[None, :] <= pair[:, None]) & below[None, :], 1, 0), axis=1) - 1
    count = rank[-1] + 1
    spot = jnp.arange(n_q * n_k + 2, dtype=jnp.int32)
    chosen = jnp.where(below, rank, -1)[None, :] == spot[:, None]
    tiles = jnp.sum(jnp.where(chosen, pair[None, :], 0), axis=1)
    tiles = jnp.where(spot == count, n_k - 1, tiles)
    return (count + count % 2).reshape(1), tiles


def in_rows(grad):
    return with_layout_constraint(grad.astype(bf16), Layout((0, 1)))


def inverse_rms(values):
    return lax.rsqrt(jnp.mean(values * values, axis=-1, keepdims=True) + EPSILON)


def norm_back(grad_norm, unit, inverse, gain):
    grad_unit = grad_norm * gain
    return inverse * (grad_unit - unit * jnp.mean(grad_unit * unit, axis=-1, keepdims=True))


def per_device(
    tokens,
    segments,
    gain_attn,
    query_scale,
    w_qkv,
    w_out,
    gain_mlp,
    w_up,
    b_up,
    w_down,
    b_down,
    cotangent,
):
    n_dp, n_ctx, n_tensor = (lax.axis_size(a) for a in ("dp", "ctx", "tensor"))
    ctx_rank, tensor_rank = lax.axis_index("ctx"), lax.axis_index("tensor")
    rows, sequences, width = tokens.shape
    shard, columns = w_qkv.shape[1:]
    local_heads = columns // HD
    group = n_ctx * n_tensor
    length = rows * group
    data = ("dp", "ctx")
    everyone = ("dp", "ctx", "tensor")
    split = local_heads % n_ctx == 0
    ctx_parts = n_ctx if split else 1
    own = local_heads // ctx_parts
    owners = ("ctx", "tensor") if split else ("tensor",)
    n_owners = ctx_parts * n_tensor
    head_width = own * 3 * HD

    inputs = tokens[:, 0].astype(f32)
    inverse_one = inverse_rms(inputs)
    unit_one = inputs * inverse_one
    normed_one = (unit_one * gain_attn).astype(bf16)

    def other_side(x):
        if n_tensor != 2:
            return lax.all_gather(x, "tensor", axis=0)
        return lax.ppermute(x, "tensor", [(0, 1), (1, 0)])

    def in_order(x, other):
        if n_tensor != 2:
            return other
        first = tensor_rank == 0
        return jnp.stack([jnp.where(first, x, other), jnp.where(first, other, x)])

    def scatter_pair(x):
        if n_tensor != 2:
            return lax.psum_scatter(x, "tensor", scatter_dimension=0, tiled=False).astype(f32)
        keep = jnp.where(tensor_rank == 0, x[0], x[1])
        send = jnp.where(tensor_rank == 0, x[1], x[0])
        return keep.astype(f32) + lax.ppermute(send, "tensor", [(0, 1), (1, 0)]).astype(f32)

    def by_distance(x, rank):
        count = x.shape[0]
        bit = 1
        while bit < count:
            y = x.reshape((count // (2 * bit), 2, bit) + x.shape[1:])
            y = jnp.where((rank & bit) > 0, jnp.flip(y, 1), y)
            x = y.reshape(x.shape)
            bit *= 2
        return x

    def exchange(x, axis, rank):
        count = x.shape[0]
        x = by_distance(x, rank)
        got = [x[0]] + [
            lax.ppermute(x[k], axis, [(i, i ^ k) for i in range(count)]) for k in range(1, count)
        ]
        return by_distance(jnp.stack(got), rank)

    qkv_rows = w_qkv.reshape(3, shard, ctx_parts, own, HD)
    for_owner = qkv_rows.transpose(2, 1, 3, 0, 4).reshape(ctx_parts, shard, head_width)
    if split:
        for_owner = exchange(for_owner, "ctx", ctx_rank)
    others = [other_side(w) for w in (w_qkv, w_out, w_up, w_down)]
    halves = [normed_one[: rows // 2], normed_one[rows // 2 :]]
    halves, for_owner, others = lax.optimization_barrier((halves, for_owner, others))
    pairs = [in_order(w, other) for w, other in zip((w_qkv, w_out, w_up, w_down), others, strict=True)]
    if split:
        owner_w = lax.all_gather(for_owner, "dp", axis=0).reshape(width, head_width)
    else:
        owner_w = lax.all_gather(for_owner[0], data, axis=0).reshape(width, head_width)

    tiles = tile_list(segments[0])
    qkv_cols = pairs[0].reshape(n_tensor, 3, shard, ctx_parts, own, HD).transpose(0, 2, 4, 3, 1, 5)
    out_cols = pairs[1].reshape(n_tensor, ctx_parts, own, HD, shard).transpose(0, 4, 2, 1, 3)

    def interleave(x, inner):
        x = x.reshape(n_tensor, shard, own * ctx_parts, inner)
        return x.transpose(1, 2, 0, 3).reshape(shard, -1)

    def side_by_side(x):
        return x.transpose(1, 0, 2).reshape(shard, -1)

    full_rows = jnp.stack(
        [
            interleave(out_cols, HD),
            side_by_side(pairs[2]),
            side_by_side(jnp.swapaxes(pairs[3], 1, 2)),
        ]
    )
    qkv_rows_full = interleave(qkv_cols, 3 * HD)
    scaling = LOG_TWO_E / math.sqrt(HD) * jax.nn.softplus(query_scale)
    scale_rows = jnp.tile(
        jnp.concatenate([scaling, jnp.ones((2 * HD,), f32)]), own
    )[:, None]

    w_rows = owner_w.T
    if group == 8 and n_tensor == 2:
        me = ctx_rank * n_tensor + tensor_rank
        spots, pieces = [], []

        def swap(x, bit):
            return lax.ppermute(x, ("ctx", "tensor"), [(i, i ^ bit) for i in range(group)])

        def add(heads_x, after, parts):
            spots.extend((distance, first) for distance, first, _ in parts)
            pieces.extend(piece for _, _, piece in parts)
            slots = jnp.stack([me ^ distance for distance, _, _ in parts])
            places = [first for _, first, _ in parts]
            shape = (group, head_width, rows)
            return project_into(heads_x, after, shape, slots, places, w_rows, scale_rows, [piece for _, _, piece in parts])

        def with_core(distance, low, high):
            return [
                (distance ^ bit, first, swap(piece, bit) if bit else piece)
                for bit in (0, 2)
                for first, piece in ((0, low), (rows // 2, high))
            ]

        own_parts = with_core(0, *halves)
        heads_x, _ = add(None, None, own_parts[:2])
        heads_x, done = add(heads_x, None, own_parts[2:])
        over_x, over_y = [swap(halves[0], 1)], [swap(halves[1], 4)]
        over_x.append(swap(halves[1], 1))
        over_y.append(swap(halves[0], 4))
        corner = [swap(over_x[0], 4), swap(over_y[0], 1)]
        over_x, over_y, full_rows, qkv_rows_full, tiles, done = lax.optimization_barrier(
            (over_x, over_y, full_rows, qkv_rows_full, tiles, done)
        )
        heads_x, done = add(heads_x, done, with_core(1, *over_x))
        heads_x, done = add(heads_x, done, with_core(4, over_y[1], over_y[0]))
        corner, done = lax.optimization_barrier((corner, done))
        heads_x, _ = add(heads_x, done, with_core(5, *corner))
    else:
        spots = None
        normed_all = lax.all_gather(normed_one, ("ctx", "tensor"), axis=0)
        heads_x = (nt(w_rows, normed_all.reshape(length, width)) * scale_rows).astype(bf16)
        heads_x = heads_x.reshape(head_width, group, rows).transpose(1, 0, 2)
    whole = lax.all_gather(full_rows, data, axis=1, tiled=True)
    out_t, up_all, down_t = whole[0], whole[1], whole[2]
    qkv_all = lax.all_gather(qkv_rows_full, data, axis=0, tiled=True)

    chunk = max(rows, BLOCK_Q, BLOCK_K)
    merge = chunk // rows
    chunks = length // chunk

    def to_chunks(x):
        if merge == 1:
            return x
        x = jnp.moveaxis(x.reshape((chunks, merge) + x.shape[1:]), 1, -2)
        return x.reshape(x.shape[:-2] + (chunk,))

    def from_chunks(x):
        if merge == 1:
            return x
        x = jnp.moveaxis(x.reshape(x.shape[:-1] + (merge, rows)), -2, 1)
        return x.reshape((group,) + x.shape[2:])

    def to_tokens(x):
        x = from_chunks(x)
        if not split:
            x = lax.dynamic_slice_in_dim(x, ctx_rank * n_tensor, n_tensor, 0)
        return lax.all_to_all(x, owners, 0, 0)

    def to_heads(x):
        x = lax.all_to_all(x, owners, 0, 0)
        if not split:
            x = lax.all_gather(x, "ctx", axis=0, tiled=True)
        return to_chunks(x)

    heads_x = to_chunks(heads_x)
    heads_x = heads_x.reshape(chunks, own, 3, HD, chunk)
    seg_chunks = segments.reshape(1, chunks, chunk)

    part = n_owners * HD

    mixed, wides, lses = [], [], []
    for p in range(own):
        o, wide, lse = attend(tiles, heads_x, seg_chunks, p)
        wides.append(wide)
        lses.append(lse)
        mixed.append(to_tokens(o).reshape(part, rows))

    hidden = inputs
    for p in range(own):
        hidden = hidden + dot(mixed[p], out_t[:, p * part : (p + 1) * part], (0,), (1,))
    inverse_two = inverse_rms(hidden)
    unit_two = hidden * inverse_two
    normed_two = (unit_two * gain_mlp).astype(bf16)
    pre_act = nn(normed_two, up_all) + b_up
    sigma = jax.nn.sigmoid(pre_act)
    activation = (pre_act * sigma).astype(bf16)
    outputs = (hidden + (nt(activation, down_t) + b_down)).astype(bf16)

    top_low = cotangent[:, 0]
    grad_top = top_low.astype(f32)
    grad_pre = (nn(top_low, down_t) * (sigma * (1 + pre_act * (1 - sigma)))).astype(bf16)
    grad_normed_two = nt(grad_pre, up_all)
    grad_hidden = grad_top + norm_back(grad_normed_two, unit_two, inverse_two, gain_mlp)
    grad_hidden_low = grad_hidden.astype(bf16)
    grad_heads = [
        nt(out_t[:, p * part : (p + 1) * part].T, grad_hidden_low).astype(bf16).reshape(n_owners, HD, rows)
        for p in range(own)
    ]
    grad_heads[0], low, act, normed, outputs = lax.optimization_barrier(
        (grad_heads[0], grad_hidden_low, activation, normed_two, outputs)
    )
    grad_heads = [to_heads(g) for g in grad_heads]
    grad_out_t = [dot(low, m, (0,), (1,)) for m in mixed]
    grad_up = dot(normed, grad_pre, (0,), (0,))
    grad_down_t = dot(top_low, act, (0,), (0,))
    stacked = jnp.concatenate([in_rows(g) for g in (*grad_out_t, grad_up, grad_down_t)], axis=1)
    stacked, qkv_all = lax.optimization_barrier((stacked, qkv_all))
    reduced = lax.psum_scatter(stacked, data, scatter_dimension=0, tiled=True)
    reduced = [reduced[:, n * width : (n + 1) * width] for n in range(3)]
    gain_two = jnp.sum(grad_normed_two * unit_two, axis=0)
    bias_up = jnp.sum(grad_pre.astype(f32), axis=0)
    bias_down = jnp.sum(grad_top, axis=0)
    scale_tile = jnp.broadcast_to(scaling[:, None], (HD, 128))
    scale_sum = jnp.zeros((HD,), f32)
    gain_part = jnp.zeros((width,), f32)
    backs, wgrads, travelled = [], [], []
    for p in range(own):
        if p:
            heads_x, grad_heads[p], wgrads[-1] = lax.optimization_barrier((heads_x, grad_heads[p], wgrads[-1]))
        dx, part_sum = attend_back(
            tiles, heads_x, grad_heads[p], wides[p], lses[p], seg_chunks, scale_tile, p
        )
        if p:
            dx, backs[-1] = lax.optimization_barrier((dx, backs[-1]))
        scale_sum = scale_sum + jnp.sum(part_sum, axis=1)
        backs.append(to_tokens(dx).reshape(3 * part, rows))
        if p == own - 1:
            grad_normed_one = jnp.zeros((rows, width), f32)
            for n in range(own - 1):
                grad_normed_one = grad_normed_one + input_grad(backs[n], qkv_all, n, ())
            dx, grad_normed_one = lax.optimization_barrier((dx, grad_normed_one))
        if spots is None:
            grad_w = lax.dot_general(
                to_chunks(jnp.swapaxes(normed_all, 1, 2)),
                dx.reshape(chunks, 3 * HD, chunk),
                (((0, 2), (0, 2)), ((), ())),
                preferred_element_type=f32,
            )
            weights_p = owner_w.reshape(width, own, 3 * HD)[:, p].astype(f32)
            gain_part = gain_part + jnp.sum(grad_w * weights_p, axis=1)
            wgrads.append(grad_w.astype(bf16))
        else:
            own_w = w_rows[p * 3 * HD : (p + 1) * 3 * HD]
            grad_w, gain_add = weight_grad(me.reshape(1), pieces, spots, own_w, dx)
            wgrads.append(grad_w.T)
            gain_part = gain_part + gain_add[0]
        if p == own - 1:
            split_out = reduced[0].reshape(shard, own, ctx_parts, n_tensor, HD).transpose(3, 0, 2, 1, 4)
            split_up, split_down = (
                reduced[n].reshape(shard, n_tensor, columns).transpose(1, 0, 2) for n in (1, 2)
            )
            mine = scatter_pair(
                jnp.stack([split_out.reshape(n_tensor, shard, columns), split_up, split_down], axis=1)
            )
            out_grad, up_grad, down_grad = mine[0].T, mine[1], mine[2].T
            wgrads[-1], gain_part, backs[-1], out_grad, up_grad, down_grad = lax.optimization_barrier(
                (wgrads[-1], gain_part, backs[-1], out_grad, up_grad, down_grad)
            )
        rows_by = by_distance(wgrads[-1].reshape(n_dp, n_ctx * shard, 3 * HD), lax.axis_index("dp"))
        wgrads[-1] = rows_by[0]
        travelled.append(
            [lax.ppermute(rows_by[k], "dp", [(i, i ^ k) for i in range(n_dp)]) for k in range(1, n_dp)]
        )
    gain_one, scale_sum = gain_part / gain_attn, scale_sum / scaling
    if not split:
        once = (ctx_rank == 0).astype(f32)
        gain_one, scale_sum = gain_one * once, scale_sum * once
    def across(x, axis):
        count = lax.axis_size(axis)
        return [x] + [lax.ppermute(x, axis, [(i, i ^ k) for i in range(count)]) for k in range(1, count)]

    sums = jnp.concatenate([gain_one, gain_two, bias_up, bias_down, scale_sum])
    small = all(n & (n - 1) == 0 and n <= 4 for n in (n_dp, n_ctx, n_tensor))
    if small:
        sums = sum(across(sums, "dp"))
    piece = jnp.concatenate(
        [sum((g.astype(f32) for g in far), w.astype(f32)).astype(bf16) for w, far in zip(wgrads, travelled, strict=True)],
        axis=1,
    )
    piece, sums = lax.optimization_barrier((piece, sums))
    piece = piece.reshape(n_ctx, shard, head_width)
    if split:
        piece = exchange(piece, "ctx", ctx_rank)
    else:
        piece = lax.dynamic_slice_in_dim(piece, ctx_rank, 1, 0)
    if small:
        sums = sum(across(sums, "ctx"))
        sums, piece = lax.optimization_barrier((sums, piece))
        sums = sum(across(sums, "tensor"))
    else:
        sums = lax.psum(sums, everyone)
    qkv_grad = piece.reshape(ctx_parts, shard, own, 3, HD).transpose(3, 1, 0, 2, 4)
    qkv_grad = qkv_grad.reshape(w_qkv.shape).astype(f32)

    grad_inputs = input_grad(
        backs[-1], qkv_all, own - 1, (grad_normed_one, tokens[:, 0], gain_attn[None], grad_hidden)
    )
    gain_one, gain_two, bias_up, bias_down = (sums[n * width : (n + 1) * width] for n in range(4))
    grad_query_scale = sums[4 * width :] * (LOG_TWO_E / math.sqrt(HD)) * jax.nn.sigmoid(query_scale)
    return (
        outputs[:, None],
        grad_inputs[:, None],
        qkv_grad,
        out_grad,
        up_grad,
        down_grad,
        gain_one,
        grad_query_scale,
        gain_two,
        bias_up,
        bias_down,
    )


def solution(mesh):
    placed = (
        P(("ctx", "tensor"), "dp", None),
        P("dp", None),
        P(),
        P(),
        P(None, ("dp", "ctx"), "tensor"),
        P("tensor", ("dp", "ctx")),
        P(),
        P(("dp", "ctx"), "tensor"),
        P(),
        P("tensor", ("dp", "ctx")),
        P(),
        P(("ctx", "tensor"), "dp", None),
    )
    return jax.shard_map(
        per_device,
        mesh=mesh,
        in_specs=placed,
        out_specs=(
            P(("ctx", "tensor"), "dp", None),
            P(("ctx", "tensor"), "dp", None),
            P(None, ("dp", "ctx"), "tensor"),
            P("tensor", ("dp", "ctx")),
            P(("dp", "ctx"), "tensor"),
            P("tensor", ("dp", "ctx")),
            P(),
            P(),
            P(),
            P(),
            P(),
        ),
        check_vma=False,
    )
```

```python
import functools
import math

import jax
import jax.numpy as jnp
from jax import lax
from jax.experimental import pallas as pl
from jax.experimental.layout import Layout, with_layout_constraint
from jax.experimental.pallas import tpu as pltpu
from jax.sharding import PartitionSpec as P

HD = 80
IDS = 32
BLOCK_Q = 512
BLOCK_K = 512
PARTS = 2
WIDE = HD + IDS
EPSILON = 1e-06
LOG_TWO_E = 1.442695041
LOG2E = 1.4426950408889634
NEGATIVE = -1e30
VMEM_BYTES = 60 << 20
bf16, f32 = jnp.bfloat16, jnp.float32


def dot(a, b, contract_a, contract_b):
    return lax.dot_general(
        a, b, ((contract_a, contract_b), ((), ())), preferred_element_type=f32
    )


def nn(a, b):
    return dot(a, b, (1,), (0,))


def nt(a, b):
    return dot(a, b, (1,), (1,))


def place(block, per, size):
    return block // per, pl.multiple_of((block % per) * size, size)


def run_tiles(length, count, tiles, prepare, process):
    n_q, n_k = length // BLOCK_Q, length // BLOCK_K

    def diagonal(t):
        t = jnp.minimum(t, n_q - 1)
        return t * n_k + t * BLOCK_Q // BLOCK_K

    def turns(number, tile, masked):
        prepare(tile(0), 0)

        def turn(t, _):
            prepare(tile(2 * t + 1), 1)
            process(tile(2 * t), 0, masked)
            prepare(tile(2 * t + 2), 0)
            process(tile(2 * t + 1), 1, masked)
            return 0

        lax.fori_loop(0, number, turn, 0)

    turns(n_q // 2, diagonal, True)
    turns(count[0] // 2, lambda t: tiles[t], False)


def attend_body(count, tiles, x_ref, segment_ref, o_ref, wide_ref, lse_ref, key_rows, query_cols, acc, top, total, scores, *, chunks, chunk):
    nk = chunks * chunk // BLOCK_K
    per_q, per_k = chunk // BLOCK_Q, chunk // BLOCK_K
    lanes = BLOCK_Q // PARTS
    for c in range(chunks):
        hot = lax.broadcasted_iota(jnp.int32, (IDS, chunk), 0) == segment_ref[0, c : c + 1, :]
        keys = jnp.concatenate([x_ref[c, 0, 1], jnp.where(hot, 1.0, 0.0).astype(bf16)], axis=0)
        key_rows[pl.ds(c * chunk, chunk), :] = keys.T
        query_cols[c] = jnp.concatenate([x_ref[c, 0, 0], jnp.where(hot, 0.0, NEGATIVE).astype(bf16)], axis=0)
        acc[c] = jnp.zeros((HD, chunk), f32)
    top[...] = jnp.full(top.shape, NEGATIVE, f32)
    total[...] = jnp.zeros(total.shape, f32)
    key_iota = lax.broadcasted_iota(jnp.int32, (BLOCK_K, lanes), 0)
    query_iota = lax.broadcasted_iota(jnp.int32, (BLOCK_K, lanes), 1)

    def prepare(tile, slot):
        c, off = place(tile // nk, per_q, BLOCK_Q)
        k = key_rows[pl.ds(pl.multiple_of((tile % nk) * BLOCK_K, BLOCK_K), BLOCK_K), :]
        for u in range(PARTS):
            scores[slot, :, u * lanes : (u + 1) * lanes] = nn(k, query_cols[c, :, pl.ds(off + u * lanes, lanes)]) * LOG2E

    def process(tile, slot, masked):
        i, j = tile // nk, tile % nk
        c, off = place(i, per_q, BLOCK_Q)
        ck_, koff = place(j, per_k, BLOCK_K)
        v = x_ref[ck_, 0, 2, :, pl.ds(koff, BLOCK_K)]
        for u in range(PARTS):
            at = pl.ds(off + u * lanes, lanes)
            row = pl.ds(c, 1)
            s = scores[slot, :, u * lanes : (u + 1) * lanes]
            if masked:
                s = jnp.where(key_iota - query_iota <= i * BLOCK_Q + u * lanes - j * BLOCK_K, s, NEGATIVE)
            old = top[row, at]
            new = jnp.maximum(old, jnp.max(s, axis=0, keepdims=True))
            p = jnp.exp2(s - new)
            shrink = jnp.exp2(old - new)
            top[row, at] = new
            total[row, at] = total[row, at] * shrink + jnp.sum(p, axis=0, keepdims=True)
            acc[c, :, at] = acc[c, :, at] * shrink + nn(v, p.astype(bf16))

    run_tiles(chunks * chunk, count, tiles, prepare, process)
    for c in range(chunks):
        t = total[c : c + 1, :]
        o = acc[c] / t
        wide_ref[c] = o
        o_ref[c] = o.astype(bf16)
        lse_ref[0, c : c + 1, :] = top[c : c + 1, :] + jnp.log2(t)


def attend_back_body(count, tiles, x_ref, g_ref, wide_ref, lse_ref, segment_ref, scale_ref, dx_ref, part_ref, key_rows, query_cols, value_rows, dq, dk, dv, delta, scores, grads, *, chunks, chunk):
    nk = chunks * chunk // BLOCK_K
    per_q, per_k = chunk // BLOCK_Q, chunk // BLOCK_K
    lanes = BLOCK_Q // PARTS
    for c in range(chunks):
        hot = lax.broadcasted_iota(jnp.int32, (IDS, chunk), 0) == segment_ref[0, c : c + 1, :]
        keys = jnp.concatenate([x_ref[c, 0, 1], jnp.where(hot, 1.0, 0.0).astype(bf16)], axis=0)
        key_rows[pl.ds(c * chunk, chunk), :] = keys.T
        query_cols[c] = jnp.concatenate([x_ref[c, 0, 0], jnp.where(hot, 0.0, NEGATIVE).astype(bf16)], axis=0)
        value_rows[pl.ds(c * chunk, chunk), :] = x_ref[c, 0, 2].T
        delta[c : c + 1, :] = jnp.sum(g_ref[c].astype(f32) * wide_ref[c], axis=0, keepdims=True)
        for ref in (dq, dk, dv):
            ref[c] = jnp.zeros((HD, chunk), f32)
    key_iota = lax.broadcasted_iota(jnp.int32, (BLOCK_K, lanes), 0)
    query_iota = lax.broadcasted_iota(jnp.int32, (BLOCK_K, lanes), 1)

    def prepare(tile, slot):
        c, off = place(tile // nk, per_q, BLOCK_Q)
        rows = pl.ds(pl.multiple_of((tile % nk) * BLOCK_K, BLOCK_K), BLOCK_K)
        k, v = key_rows[rows, :], value_rows[rows, :]
        for u in range(PARTS):
            at = pl.ds(off + u * lanes, lanes)
            scores[slot, :, u * lanes : (u + 1) * lanes] = nn(k, query_cols[c, :, at])
            grads[slot, :, u * lanes : (u + 1) * lanes] = nn(v, g_ref[c, :, at])

    def process(tile, slot, masked):
        i, j = tile // nk, tile % nk
        c, off = place(i, per_q, BLOCK_Q)
        kc, koff = place(j, per_k, BLOCK_K)
        kat = pl.ds(koff, BLOCK_K)
        kt = x_ref[kc, 0, 1, :, kat]
        for u in range(PARTS):
            at = pl.ds(off + u * lanes, lanes)
            row = pl.ds(c, 1)
            s = scores[slot, :, u * lanes : (u + 1) * lanes] * LOG2E
            if masked:
                s = jnp.where(key_iota - query_iota <= i * BLOCK_Q + u * lanes - j * BLOCK_K, s, NEGATIVE)
            p = jnp.exp2(s - lse_ref[0, row, at])
            low = (p * (grads[slot, :, u * lanes : (u + 1) * lanes] - delta[row, at])).astype(bf16)
            q, g = x_ref[c, 0, 0, :, at], g_ref[c, :, at]
            dv[kc, :, kat] += nt(g, p.astype(bf16))
            dk[kc, :, kat] += nt(q, low)
            dq[c, :, at] += nn(kt, low)

    run_tiles(chunks * chunk, count, tiles, prepare, process)
    part = jnp.zeros((HD, 128), f32)
    for c in range(chunks):
        grad = dq[c]
        dx_ref[c, 0] = (grad * scale_ref[:, 0:1]).astype(bf16)
        dx_ref[c, 1] = dk[c].astype(bf16)
        dx_ref[c, 2] = dv[c].astype(bf16)
        term = grad * x_ref[c, 0, 0].astype(f32)
        for u in range(chunk // 128):
            part = part + term[:, u * 128 : (u + 1) * 128]
    part_ref[...] = part


def kernel_cost(length, matmuls):
    pairs = length * 2048
    return pl.CostEstimate(
        flops=matmuls * 512 * pairs, bytes_accessed=length * 2048, transcendentals=pairs
    )


def attend(tables, x, segments, p):
    chunks, _, _, _, chunk = x.shape
    flat = lambda g, *_: (0, 0, 0)
    return pl.pallas_call(
        functools.partial(attend_body, chunks=chunks, chunk=chunk),
        grid_spec=pltpu.PrefetchScalarGridSpec(
            num_scalar_prefetch=2,
            grid=(1,),
            in_specs=[
                pl.BlockSpec((chunks, 1, 3, HD, chunk), lambda g, *_: (0, p, 0, 0, 0)),
                pl.BlockSpec((1, chunks, chunk), flat),
            ],
            out_specs=[
                pl.BlockSpec((chunks, HD, chunk), flat),
                pl.BlockSpec((chunks, HD, chunk), flat),
                pl.BlockSpec((1, chunks, chunk), flat),
            ],
            scratch_shapes=[
                pltpu.VMEM((chunks * chunk, WIDE), bf16),
                pltpu.VMEM((chunks, WIDE, chunk), bf16),
                pltpu.VMEM((chunks, HD, chunk), f32),
                pltpu.VMEM((chunks, chunk), f32),
                pltpu.VMEM((chunks, chunk), f32),
                pltpu.VMEM((2, BLOCK_K, BLOCK_Q), f32),
            ],
        ),
        out_shape=[
            jax.ShapeDtypeStruct((chunks, HD, chunk), bf16),
            jax.ShapeDtypeStruct((chunks, HD, chunk), f32),
            jax.ShapeDtypeStruct((1, chunks, chunk), f32),
        ],
        compiler_params=pltpu.CompilerParams(vmem_limit_bytes=VMEM_BYTES),
        cost_estimate=kernel_cost(chunks * chunk, 2),
        name="attend",
    )(*tables, x, segments)


def attend_back(tables, x, grad, wide, lse, segments, scale, p):
    chunks, _, _, _, chunk = x.shape
    flat = lambda g, *_: (0, 0, 0)
    return pl.pallas_call(
        functools.partial(attend_back_body, chunks=chunks, chunk=chunk),
        grid_spec=pltpu.PrefetchScalarGridSpec(
            num_scalar_prefetch=2,
            grid=(1,),
            in_specs=[
                pl.BlockSpec((chunks, 1, 3, HD, chunk), lambda g, *_: (0, p, 0, 0, 0)),
                pl.BlockSpec((chunks, HD, chunk), flat),
                pl.BlockSpec((chunks, HD, chunk), flat),
                pl.BlockSpec((1, chunks, chunk), flat),
                pl.BlockSpec((1, chunks, chunk), flat),
                pl.BlockSpec((HD, 128), lambda g, *_: (0, 0)),
            ],
            out_specs=[
                pl.BlockSpec((chunks, 3, HD, chunk), lambda g, *_: (0, 0, 0, 0)),
                pl.BlockSpec((HD, 128), lambda g, *_: (0, 0)),
            ],
            scratch_shapes=[
                pltpu.VMEM((chunks * chunk, WIDE), bf16),
                pltpu.VMEM((chunks, WIDE, chunk), bf16),
                pltpu.VMEM((chunks * chunk, HD), bf16),
                pltpu.VMEM((chunks, HD, chunk), f32),
                pltpu.VMEM((chunks, HD, chunk), f32),
                pltpu.VMEM((chunks, HD, chunk), f32),
                pltpu.VMEM((chunks, chunk), f32),
                pltpu.VMEM((2, BLOCK_K, BLOCK_Q), f32),
                pltpu.VMEM((2, BLOCK_K, BLOCK_Q), f32),
            ],
        ),
        out_shape=[
            jax.ShapeDtypeStruct((chunks, 3, HD, chunk), bf16),
            jax.ShapeDtypeStruct((HD, 128), f32),
        ],
        compiler_params=pltpu.CompilerParams(vmem_limit_bytes=VMEM_BYTES),
        cost_estimate=kernel_cost(chunks * chunk, 5),
        name="attend_back",
    )(*tables, x, grad, wide, lse, segments, scale)


def project_body(slots_ref, w_ref, scale_ref, *refs, places):
    n = len(places)
    pieces, (out_ref, done_ref, buffers, results, in_sems, out_sems) = refs[:n], refs[-6:]
    done_ref[...] = jnp.zeros(done_ref.shape, f32)

    def fetch(i):
        return pltpu.make_async_copy(pieces[i], buffers.at[i], in_sems.at[i])

    def store(i):
        first, rows = places[i], results.shape[2]
        return pltpu.make_async_copy(
            results.at[i], out_ref.at[slots_ref[i], :, pl.ds(first, rows)], out_sems.at[i]
        )

    for i in range(n):
        fetch(i).start()
    for i in range(n):
        fetch(i).wait()
        results[i] = (nt(w_ref[...], buffers[i]) * scale_ref[...]).astype(bf16)
        store(i).start()
    for i in range(n):
        store(i).wait()


def project_into(heads, after, shape, slots, places, w, scale, pieces):
    features, width = w.shape
    n, rows = len(pieces), pieces[0].shape[0]
    kept = [] if heads is None else [heads]
    tail = [] if after is None else [after]
    whole = pl.BlockSpec(memory_space=pltpu.VMEM)
    anywhere = pl.BlockSpec(memory_space=pl.ANY)
    return pl.pallas_call(
        functools.partial(project_body, places=places),
        in_specs=[pl.BlockSpec(memory_space=pltpu.SMEM), whole, whole] + [anywhere] * (n + len(kept) + len(tail)),
        out_specs=[anywhere, whole],
        out_shape=[jax.ShapeDtypeStruct(shape, bf16), jax.ShapeDtypeStruct((8, 128), f32)],
        scratch_shapes=[
            pltpu.VMEM((n, rows, width), bf16),
            pltpu.VMEM((n, features, rows), bf16),
            pltpu.SemaphoreType.DMA((n,)),
            pltpu.SemaphoreType.DMA((n,)),
        ],
        input_output_aliases={3 + n: 0} if kept else {},
        compiler_params=pltpu.CompilerParams(vmem_limit_bytes=VMEM_BYTES),
        cost_estimate=pl.CostEstimate(
            flops=2 * n * features * width * rows, bytes_accessed=4 * n * width * rows, transcendentals=0
        ),
        name="project",
    )(slots, w, scale, *pieces, *kept, *tail)


def weight_grad_body(me_ref, *refs, spots):
    n = len(spots)
    pieces, (w_ref, dx, out_ref, gain_ref, buffers, acc, sems) = refs[:n], refs[n:]
    rows, width = buffers.shape[1:]

    def copy(i):
        return pltpu.make_async_copy(pieces[i], buffers.at[i], sems.at[i])

    for i in range(n):
        copy(i).start()
    for i, (distance, first) in enumerate(spots):
        part_dx = dx[me_ref[0] ^ distance, :, :, first : first + rows]
        part_dx = part_dx.reshape(part_dx.shape[0] * part_dx.shape[1], rows)
        copy(i).wait()
        for lane in range(0, width, 256):
            part = nn(part_dx, buffers[i, :, lane : lane + 256])
            acc[:, lane : lane + 256] = part + acc[:, lane : lane + 256] if i else part
    total = acc[...]
    out_ref[...] = total.astype(bf16)
    gain_ref[...] = jnp.sum(total * w_ref[...].astype(f32), axis=0, keepdims=True)


def weight_grad(me, pieces, spots, w, dx):
    features, width = w.shape
    whole = pl.BlockSpec(memory_space=pltpu.VMEM)
    return pl.pallas_call(
        functools.partial(weight_grad_body, spots=spots),
        in_specs=[pl.BlockSpec(memory_space=pltpu.SMEM)]
        + [pl.BlockSpec(memory_space=pl.ANY)] * len(pieces)
        + [whole] * 2,
        out_specs=[whole, whole],
        out_shape=[
            jax.ShapeDtypeStruct((features, width), bf16),
            jax.ShapeDtypeStruct((1, width), f32),
        ],
        scratch_shapes=[
            pltpu.VMEM((len(pieces),) + pieces[0].shape, bf16),
            pltpu.VMEM((features, width), f32),
            pltpu.SemaphoreType.DMA((len(pieces),)),
        ],
        compiler_params=pltpu.CompilerParams(vmem_limit_bytes=VMEM_BYTES),
        cost_estimate=pl.CostEstimate(flops=1, bytes_accessed=1, transcendentals=0),
        name="weight_grad",
    )(me, *pieces, w, dx)


def back_one_body(back_ref, w_ref, out_ref):
    out_ref[...] = nn(w_ref[...], back_ref[...]).T


def finish_body(back_ref, w_ref, other_ref, tokens_ref, gain_ref, hidden_ref, out_ref):
    grad_normed = other_ref[...] + nn(w_ref[...], back_ref[...]).T
    inputs = tokens_ref[...].astype(f32)
    inverse = inverse_rms(inputs)
    out_ref[...] = (
        hidden_ref[...] + norm_back(grad_normed, inputs * inverse, inverse, gain_ref[...])
    ).astype(bf16)


def input_grad(back, w, p, others):
    features, rows = back.shape
    width = w.shape[0]
    block = math.gcd(rows, 256)
    by_tokens = pl.BlockSpec((block, width), lambda t: (t, 0))
    specs = [by_tokens, by_tokens, pl.BlockSpec((1, width), lambda t: (0, 0)), by_tokens] if others else []
    return pl.pallas_call(
        finish_body if others else back_one_body,
        grid=(rows // block,),
        in_specs=[
            pl.BlockSpec((features, block), lambda t: (0, t)),
            pl.BlockSpec((width, features), lambda t: (0, p)),
        ]
        + specs,
        out_specs=by_tokens,
        out_shape=jax.ShapeDtypeStruct((rows, width), bf16 if others else f32),
        compiler_params=pltpu.CompilerParams(vmem_limit_bytes=VMEM_BYTES),
        cost_estimate=pl.CostEstimate(
            flops=2 * features * width * rows if others else 1,
            bytes_accessed=16 * width * rows if others else 1,
            transcendentals=0,
        ),
        name="input_grad",
    )(back, w, *others)


def head_grad_body(low_ref, w_ref, out_ref):
    out_ref[...] = nn(low_ref[...], w_ref[0]).T.astype(bf16)


def head_grad(low, whole, p, features):
    rows, width = low.shape
    block = math.gcd(rows, 256)
    return pl.pallas_call(
        head_grad_body,
        grid=(rows // block,),
        in_specs=[
            pl.BlockSpec((block, width), lambda t: (t, 0)),
            pl.BlockSpec((1, width, features), lambda t: (0, 0, p)),
        ],
        out_specs=pl.BlockSpec((features, block), lambda t: (0, t)),
        out_shape=jax.ShapeDtypeStruct((features, rows), bf16),
        compiler_params=pltpu.CompilerParams(vmem_limit_bytes=VMEM_BYTES),
        cost_estimate=pl.CostEstimate(flops=1, bytes_accessed=1, transcendentals=0),
        name="head_grad",
    )(low, whole)


def outputs_body(act_ref, w_ref, hidden_ref, bias_ref, out_ref):
    out_ref[...] = (hidden_ref[...] + (nt(act_ref[...], w_ref[0]) + bias_ref[...])).astype(bf16)


def down_outputs(act, whole, hidden, bias):
    rows, width = hidden.shape
    block = math.gcd(rows, 256)
    by_tokens = lambda n: pl.BlockSpec((block, n), lambda t: (t, 0))
    return pl.pallas_call(
        outputs_body,
        grid=(rows // block,),
        in_specs=[
            by_tokens(act.shape[1]),
            pl.BlockSpec((1, width, act.shape[1]), lambda t: (2, 0, 0)),
            by_tokens(width),
            pl.BlockSpec((1, width), lambda t: (0, 0)),
        ],
        out_specs=by_tokens(width),
        out_shape=jax.ShapeDtypeStruct((rows, width), bf16),
        compiler_params=pltpu.CompilerParams(vmem_limit_bytes=VMEM_BYTES),
        cost_estimate=pl.CostEstimate(flops=1, bytes_accessed=1, transcendentals=0),
        name="outputs",
    )(act, whole, hidden, bias[None])


def tile_list(segments):
    length = segments.shape[0]
    n_q, n_k = length // BLOCK_Q, length // BLOCK_K
    first = jnp.sum(segments[None, :] < segments[::BLOCK_Q][:, None], axis=1, dtype=jnp.int32)[:, None]
    q_block = jnp.arange(n_q, dtype=jnp.int32)[:, None]
    k_last = jnp.arange(n_k, dtype=jnp.int32)[None, :] * BLOCK_K + BLOCK_K - 1
    below = ((k_last < q_block * BLOCK_Q) & (k_last >= first)).reshape(-1)
    pair = jnp.arange(n_q * n_k, dtype=jnp.int32)
    rank = jnp.sum(jnp.where((pair[None, :] <= pair[:, None]) & below[None, :], 1, 0), axis=1) - 1
    count = rank[-1] + 1
    spot = jnp.arange(n_q * n_k + 2, dtype=jnp.int32)
    chosen = jnp.where(below, rank, -1)[None, :] == spot[:, None]
    tiles = jnp.sum(jnp.where(chosen, pair[None, :], 0), axis=1)
    tiles = jnp.where(spot == count, n_k - 1, tiles)
    return (count + count % 2).reshape(1), tiles


def in_rows(grad):
    return with_layout_constraint(grad.astype(bf16), Layout((0, 1)))


def inverse_rms(values):
    return lax.rsqrt(jnp.mean(values * values, axis=-1, keepdims=True) + EPSILON)


def norm_back(grad_norm, unit, inverse, gain):
    grad_unit = grad_norm * gain
    return inverse * (grad_unit - unit * jnp.mean(grad_unit * unit, axis=-1, keepdims=True))


def per_device(
    tokens,
    segments,
    gain_attn,
    query_scale,
    w_qkv,
    w_out,
    gain_mlp,
    w_up,
    b_up,
    w_down,
    b_down,
    cotangent,
):
    n_dp, n_ctx, n_tensor = (lax.axis_size(a) for a in ("dp", "ctx", "tensor"))
    ctx_rank, tensor_rank = lax.axis_index("ctx"), lax.axis_index("tensor")
    rows, sequences, width = tokens.shape
    shard, columns = w_qkv.shape[1:]
    local_heads = columns // HD
    group = n_ctx * n_tensor
    length = rows * group
    data = ("dp", "ctx")
    everyone = ("dp", "ctx", "tensor")
    split = local_heads % n_ctx == 0
    ctx_parts = n_ctx if split else 1
    own = local_heads // ctx_parts
    owners = ("ctx", "tensor") if split else ("tensor",)
    n_owners = ctx_parts * n_tensor
    head_width = own * 3 * HD

    inputs = tokens[:, 0].astype(f32)
    inverse_one = inverse_rms(inputs)
    unit_one = inputs * inverse_one
    normed_one = (unit_one * gain_attn).astype(bf16)

    def other_side(x):
        if n_tensor != 2:
            return lax.all_gather(x, "tensor", axis=0)
        return lax.ppermute(x, "tensor", [(0, 1), (1, 0)])

    def in_order(x, other):
        if n_tensor != 2:
            return other
        first = tensor_rank == 0
        return jnp.stack([jnp.where(first, x, other), jnp.where(first, other, x)])

    def scatter_pair(x):
        if n_tensor != 2:
            return lax.psum_scatter(x, "tensor", scatter_dimension=0, tiled=False).astype(f32)
        keep = jnp.where(tensor_rank == 0, x[0], x[1])
        send = jnp.where(tensor_rank == 0, x[1], x[0])
        return keep.astype(f32) + lax.ppermute(send, "tensor", [(0, 1), (1, 0)]).astype(f32)

    def by_distance(x, rank):
        count = x.shape[0]
        bit = 1
        while bit < count:
            y = x.reshape((count // (2 * bit), 2, bit) + x.shape[1:])
            y = jnp.where((rank & bit) > 0, jnp.flip(y, 1), y)
            x = y.reshape(x.shape)
            bit *= 2
        return x

    def exchange(x, axis, rank):
        count = x.shape[0]
        x = by_distance(x, rank)
        got = [x[0]] + [
            lax.ppermute(x[k], axis, [(i, i ^ k) for i in range(count)]) for k in range(1, count)
        ]
        return by_distance(jnp.stack(got), rank)

    qkv_rows = w_qkv.reshape(3, shard, ctx_parts, own, HD)
    for_owner = qkv_rows.transpose(2, 1, 3, 0, 4).reshape(ctx_parts, shard, head_width)
    if split:
        for_owner = exchange(for_owner, "ctx", ctx_rank)
    others = [other_side(w) for w in (w_qkv, w_out, w_up, w_down)]
    halves = [normed_one[: rows // 2], normed_one[rows // 2 :]]
    halves, for_owner, others = lax.optimization_barrier((halves, for_owner, others))
    pairs = [in_order(w, other) for w, other in zip((w_qkv, w_out, w_up, w_down), others, strict=True)]
    if split:
        owner_w = lax.all_gather(for_owner, "dp", axis=0).reshape(width, head_width)
    else:
        owner_w = lax.all_gather(for_owner[0], data, axis=0).reshape(width, head_width)

    tiles = tile_list(segments[0])
    qkv_cols = pairs[0].reshape(n_tensor, 3, shard, ctx_parts, own, HD).transpose(0, 2, 4, 3, 1, 5)
    out_cols = pairs[1].reshape(n_tensor, ctx_parts, own, HD, shard).transpose(0, 4, 2, 1, 3)

    def interleave(x, inner):
        x = x.reshape(n_tensor, shard, own * ctx_parts, inner)
        return x.transpose(1, 2, 0, 3).reshape(shard, -1)

    def side_by_side(x):
        return x.transpose(1, 0, 2).reshape(shard, -1)

    full_rows = jnp.stack(
        [
            interleave(out_cols, HD),
            side_by_side(pairs[2]),
            side_by_side(jnp.swapaxes(pairs[3], 1, 2)),
        ]
    )
    qkv_rows_full = interleave(qkv_cols, 3 * HD)
    scaling = LOG_TWO_E / math.sqrt(HD) * jax.nn.softplus(query_scale)
    scale_rows = jnp.tile(
        jnp.concatenate([scaling, jnp.ones((2 * HD,), f32)]), own
    )[:, None]

    w_rows = owner_w.T
    if group == 8 and n_tensor == 2:
        me = ctx_rank * n_tensor + tensor_rank
        spots, pieces = [], []

        def swap(x, bit):
            return lax.ppermute(x, ("ctx", "tensor"), [(i, i ^ bit) for i in range(group)])

        def add(heads_x, after, parts):
            spots.extend((distance, first) for distance, first, _ in parts)
            pieces.extend(piece for _, _, piece in parts)
            slots = jnp.stack([me ^ distance for distance, _, _ in parts])
            places = [first for _, first, _ in parts]
            shape = (group, head_width, rows)
            return project_into(heads_x, after, shape, slots, places, w_rows, scale_rows, [piece for _, _, piece in parts])

        def with_core(distance, low, high):
            return [
                (distance ^ bit, first, swap(piece, bit) if bit else piece)
                for bit in (0, 2)
                for first, piece in ((0, low), (rows // 2, high))
            ]

        own_parts = with_core(0, *halves)
        heads_x, _ = add(None, None, own_parts[:2])
        heads_x, done = add(heads_x, None, own_parts[2:])
        over_x, over_y = [swap(halves[0], 1)], [swap(halves[1], 4)]
        over_x.append(swap(halves[1], 1))
        over_y.append(swap(halves[0], 4))
        corner = [swap(over_x[0], 4), swap(over_y[0], 1)]
        over_x, over_y, full_rows, qkv_rows_full, tiles, done = lax.optimization_barrier(
            (over_x, over_y, full_rows, qkv_rows_full, tiles, done)
        )
        heads_x, done = add(heads_x, done, with_core(1, *over_x))
        heads_x, done = add(heads_x, done, with_core(4, over_y[1], over_y[0]))
        corner, done = lax.optimization_barrier((corner, done))
        heads_x, _ = add(heads_x, done, with_core(5, *corner))
    else:
        spots = None
        normed_all = lax.all_gather(normed_one, ("ctx", "tensor"), axis=0)
        heads_x = (nt(w_rows, normed_all.reshape(length, width)) * scale_rows).astype(bf16)
        heads_x = heads_x.reshape(head_width, group, rows).transpose(1, 0, 2)
    whole = lax.all_gather(full_rows, data, axis=1, tiled=True)
    out_t, up_all, down_t = whole[0], whole[1], whole[2]
    qkv_all = lax.all_gather(qkv_rows_full, data, axis=0, tiled=True)

    chunk = max(rows, BLOCK_Q, BLOCK_K)
    merge = chunk // rows
    chunks = length // chunk

    def to_chunks(x):
        if merge == 1:
            return x
        x = jnp.moveaxis(x.reshape((chunks, merge) + x.shape[1:]), 1, -2)
        return x.reshape(x.shape[:-2] + (chunk,))

    def from_chunks(x):
        if merge == 1:
            return x
        x = jnp.moveaxis(x.reshape(x.shape[:-1] + (merge, rows)), -2, 1)
        return x.reshape((group,) + x.shape[2:])

    def to_tokens(x):
        x = from_chunks(x)
        if not split:
            x = lax.dynamic_slice_in_dim(x, ctx_rank * n_tensor, n_tensor, 0)
        return lax.all_to_all(x, owners, 0, 0)

    def to_heads(x):
        x = lax.all_to_all(x, owners, 0, 0)
        if not split:
            x = lax.all_gather(x, "ctx", axis=0, tiled=True)
        return to_chunks(x)

    heads_x = to_chunks(heads_x)
    heads_x = heads_x.reshape(chunks, own, 3, HD, chunk)
    seg_chunks = segments.reshape(1, chunks, chunk)

    part = n_owners * HD

    mixed, wides, lses = [], [], []
    for p in range(own):
        o, wide, lse = attend(tiles, heads_x, seg_chunks, p)
        wides.append(wide)
        lses.append(lse)
        mixed.append(to_tokens(o).reshape(part, rows))

    hidden = inputs
    for p in range(own):
        hidden = hidden + dot(mixed[p], out_t[:, p * part : (p + 1) * part], (0,), (1,))
    inverse_two = inverse_rms(hidden)
    unit_two = hidden * inverse_two
    normed_two = (unit_two * gain_mlp).astype(bf16)
    pre_act = nn(normed_two, up_all) + b_up
    sigma = jax.nn.sigmoid(pre_act)
    activation = (pre_act * sigma).astype(bf16)
    top_low = cotangent[:, 0]
    grad_top = top_low.astype(f32)
    grad_pre = (nn(top_low, down_t) * (sigma * (1 + pre_act * (1 - sigma)))).astype(bf16)
    grad_normed_two = nt(grad_pre, up_all)
    grad_hidden = grad_top + norm_back(grad_normed_two, unit_two, inverse_two, gain_mlp)
    grad_hidden_low = grad_hidden.astype(bf16)
    grad_heads = [nt(out_t[:, :part].T, grad_hidden_low).astype(bf16)]
    grad_heads += [head_grad(grad_hidden_low, whole, p, part) for p in range(1, own)]
    grad_heads = [g.reshape(n_owners, HD, rows) for g in grad_heads]
    grad_heads[0], low, act, normed = lax.optimization_barrier(
        (grad_heads[0], grad_hidden_low, activation, normed_two)
    )
    outputs = down_outputs(act, whole, hidden, b_down)
    grad_heads[-1], outputs = lax.optimization_barrier((grad_heads[-1], outputs))
    grad_heads = [to_heads(g) for g in grad_heads]
    grad_out_t = [dot(low, m, (0,), (1,)) for m in mixed]
    grad_up = dot(normed, grad_pre, (0,), (0,))
    grad_down_t = dot(top_low, act, (0,), (0,))
    stacked = jnp.concatenate([in_rows(g) for g in (*grad_out_t, grad_up, grad_down_t)], axis=1)
    stacked, qkv_all = lax.optimization_barrier((stacked, qkv_all))
    reduced = lax.psum_scatter(stacked, data, scatter_dimension=0, tiled=True)
    reduced = [reduced[:, n * width : (n + 1) * width] for n in range(3)]
    gain_two = jnp.sum(grad_normed_two * unit_two, axis=0)
    bias_up = jnp.sum(grad_pre.astype(f32), axis=0)
    bias_down = jnp.sum(grad_top, axis=0)
    scale_tile = jnp.broadcast_to(scaling[:, None], (HD, 128))
    scale_sum = jnp.zeros((HD,), f32)
    gain_part = jnp.zeros((width,), f32)
    dxs, backs, wgrads, travelled = [], [], [], []
    for p in range(own):
        dx, part_sum = attend_back(
            tiles, heads_x, grad_heads[p], wides[p], lses[p], seg_chunks, scale_tile, p
        )
        if p:
            dx, backs[-1] = lax.optimization_barrier((dx, backs[-1]))
        scale_sum = scale_sum + jnp.sum(part_sum, axis=1)
        backs.append(to_tokens(dx).reshape(3 * part, rows))
        dxs.append(dx)
    dxs = lax.optimization_barrier(dxs)
    for p, dx in enumerate(dxs):
        if p == own - 1:
            grad_normed_one = jnp.zeros((rows, width), f32)
            for n in range(own - 1):
                backs[n], wgrads[n] = lax.optimization_barrier((backs[n], wgrads[n]))
                grad_normed_one = grad_normed_one + input_grad(backs[n], qkv_all, n, ())
            dx, grad_normed_one = lax.optimization_barrier((dx, grad_normed_one))
        if spots is None:
            grad_w = lax.dot_general(
                to_chunks(jnp.swapaxes(normed_all, 1, 2)),
                dx.reshape(chunks, 3 * HD, chunk),
                (((0, 2), (0, 2)), ((), ())),
                preferred_element_type=f32,
            )
            weights_p = owner_w.reshape(width, own, 3 * HD)[:, p].astype(f32)
            gain_part = gain_part + jnp.sum(grad_w * weights_p, axis=1)
            wgrads.append(grad_w.astype(bf16))
        else:
            own_w = w_rows[p * 3 * HD : (p + 1) * 3 * HD]
            grad_w, gain_add = weight_grad(me.reshape(1), pieces, spots, own_w, dx)
            wgrads.append(grad_w.T)
            gain_part = gain_part + gain_add[0]
        if p == own - 1:
            split_out = reduced[0].reshape(shard, own, ctx_parts, n_tensor, HD).transpose(3, 0, 2, 1, 4)
            split_up, split_down = (
                reduced[n].reshape(shard, n_tensor, columns).transpose(1, 0, 2) for n in (1, 2)
            )
            halves_of = jnp.stack([split_out.reshape(n_tensor, shard, columns), split_up, split_down], axis=1)
            wgrads[-1], gain_part, backs[-1], halves_of, travelled = lax.optimization_barrier(
                (wgrads[-1], gain_part, backs[-1], halves_of, travelled)
            )
        rows_by = by_distance(wgrads[-1].reshape(n_dp, n_ctx * shard, 3 * HD), lax.axis_index("dp"))
        wgrads[-1] = rows_by[0]
        travelled.append(
            [lax.ppermute(rows_by[k], "dp", [(i, i ^ k) for i in range(n_dp)]) for k in range(1, n_dp)]
        )
    gain_one, scale_sum = gain_part / gain_attn, scale_sum / scaling
    if not split:
        once = (ctx_rank == 0).astype(f32)
        gain_one, scale_sum = gain_one * once, scale_sum * once

    def doubled(x, axis):
        count, bit = lax.axis_size(axis), 1
        while bit < count:
            x = x + lax.ppermute(x, axis, [(i, i ^ bit) for i in range(count)])
            bit *= 2
        return x

    sums = jnp.concatenate([gain_one, gain_two, bias_up, bias_down, scale_sum])
    small = all(n & (n - 1) == 0 and n <= 4 for n in (n_dp, n_ctx, n_tensor))
    if small:
        sums = doubled(sums, "dp")
    piece = jnp.concatenate(
        [sum((g.astype(f32) for g in far), w.astype(f32)).astype(bf16) for w, far in zip(wgrads, travelled, strict=True)],
        axis=1,
    )
    grad_inputs = input_grad(
        backs[-1], qkv_all, own - 1, (grad_normed_one, tokens[:, 0], gain_attn[None], grad_hidden)
    )
    mine = scatter_pair(halves_of)
    piece, sums, grad_inputs, mine = lax.optimization_barrier((piece, sums, grad_inputs, mine))
    out_grad, up_grad, down_grad = mine[0].T, mine[1], mine[2].T
    piece = piece.reshape(n_ctx, shard, head_width)
    if split:
        piece = exchange(piece, "ctx", ctx_rank)
    else:
        piece = lax.dynamic_slice_in_dim(piece, ctx_rank, 1, 0)
    if small:
        sums = doubled(sums, "ctx")
        sums, piece = lax.optimization_barrier((sums, piece))
        sums = doubled(sums, "tensor")
    else:
        sums = lax.psum(sums, everyone)
    qkv_grad = piece.reshape(ctx_parts, shard, own, 3, HD).transpose(3, 1, 0, 2, 4)
    qkv_grad = qkv_grad.reshape(w_qkv.shape).astype(f32)

    gain_one, gain_two, bias_up, bias_down = (sums[n * width : (n + 1) * width] for n in range(4))
    grad_query_scale = sums[4 * width :] * (LOG_TWO_E / math.sqrt(HD)) * jax.nn.sigmoid(query_scale)
    return (
        outputs[:, None],
        grad_inputs[:, None],
        qkv_grad,
        out_grad,
        up_grad,
        down_grad,
        gain_one,
        grad_query_scale,
        gain_two,
        bias_up,
        bias_down,
    )


def solution(mesh):
    placed = (
        P(("ctx", "tensor"), "dp", None),
        P("dp", None),
        P(),
        P(),
        P(None, ("dp", "ctx"), "tensor"),
        P("tensor", ("dp", "ctx")),
        P(),
        P(("dp", "ctx"), "tensor"),
        P(),
        P("tensor", ("dp", "ctx")),
        P(),
        P(("ctx", "tensor"), "dp", None),
    )
    return jax.shard_map(
        per_device,
        mesh=mesh,
        in_specs=placed,
        out_specs=(
            P(("ctx", "tensor"), "dp", None),
            P(("ctx", "tensor"), "dp", None),
            P(None, ("dp", "ctx"), "tensor"),
            P("tensor", ("dp", "ctx")),
            P(("dp", "ctx"), "tensor"),
            P("tensor", ("dp", "ctx")),
            P(),
            P(),
            P(),
            P(),
            P(),
        ),
        check_vma=False,
    )
```

```python
import functools
import math

import jax
import jax.numpy as jnp
from jax import lax
from jax.experimental import pallas as pl
from jax.experimental.layout import Layout, with_layout_constraint
from jax.experimental.pallas import tpu as pltpu
from jax.sharding import PartitionSpec as P

HD = 80
IDS = 32
BLOCK_Q = 512
BLOCK_K = 512
PARTS = 2
WIDE = HD + IDS
EPSILON = 1e-06
LOG_TWO_E = 1.442695041
LOG2E = 1.4426950408889634
NEGATIVE = -1e30
VMEM_BYTES = 60 << 20
bf16, f32 = jnp.bfloat16, jnp.float32


def dot(a, b, contract_a, contract_b):
    return lax.dot_general(
        a, b, ((contract_a, contract_b), ((), ())), preferred_element_type=f32
    )


def nn(a, b):
    return dot(a, b, (1,), (0,))


def nt(a, b):
    return dot(a, b, (1,), (1,))


def place(block, per, size):
    return block // per, pl.multiple_of((block % per) * size, size)


def run_tiles(length, count, tiles, prepare, process):
    n_q, n_k = length // BLOCK_Q, length // BLOCK_K

    def diagonal(t):
        t = jnp.minimum(t, n_q - 1)
        return t * n_k + t * BLOCK_Q // BLOCK_K

    def turns(number, tile, masked):
        prepare(tile(0), 0)

        def turn(t, _):
            prepare(tile(2 * t + 1), 1)
            process(tile(2 * t), 0, masked)
            prepare(tile(2 * t + 2), 0)
            process(tile(2 * t + 1), 1, masked)
            return 0

        lax.fori_loop(0, number, turn, 0)

    turns(n_q // 2, diagonal, True)
    turns(count[0] // 2, lambda t: tiles[t], False)


def attend_body(count, tiles, x_ref, segment_ref, o_ref, wide_ref, lse_ref, key_rows, query_cols, acc, top, total, scores, *, chunks, chunk):
    nk = chunks * chunk // BLOCK_K
    per_q, per_k = chunk // BLOCK_Q, chunk // BLOCK_K
    lanes = BLOCK_Q // PARTS
    for c in range(chunks):
        hot = lax.broadcasted_iota(jnp.int32, (IDS, chunk), 0) == segment_ref[0, c : c + 1, :]
        keys = jnp.concatenate([x_ref[c, 0, 1], jnp.where(hot, 1.0, 0.0).astype(bf16)], axis=0)
        key_rows[pl.ds(c * chunk, chunk), :] = keys.T
        query_cols[c] = jnp.concatenate([x_ref[c, 0, 0], jnp.where(hot, 0.0, NEGATIVE).astype(bf16)], axis=0)
        acc[c] = jnp.zeros((HD, chunk), f32)
    top[...] = jnp.full(top.shape, NEGATIVE, f32)
    total[...] = jnp.zeros(total.shape, f32)
    key_iota = lax.broadcasted_iota(jnp.int32, (BLOCK_K, lanes), 0)
    query_iota = lax.broadcasted_iota(jnp.int32, (BLOCK_K, lanes), 1)

    def prepare(tile, slot):
        c, off = place(tile // nk, per_q, BLOCK_Q)
        k = key_rows[pl.ds(pl.multiple_of((tile % nk) * BLOCK_K, BLOCK_K), BLOCK_K), :]
        for u in range(PARTS):
            scores[slot, :, u * lanes : (u + 1) * lanes] = nn(k, query_cols[c, :, pl.ds(off + u * lanes, lanes)]) * LOG2E

    def process(tile, slot, masked):
        i, j = tile // nk, tile % nk
        c, off = place(i, per_q, BLOCK_Q)
        ck_, koff = place(j, per_k, BLOCK_K)
        v = x_ref[ck_, 0, 2, :, pl.ds(koff, BLOCK_K)]
        for u in range(PARTS):
            at = pl.ds(off + u * lanes, lanes)
            row = pl.ds(c, 1)
            s = scores[slot, :, u * lanes : (u + 1) * lanes]
            if masked:
                s = jnp.where(key_iota - query_iota <= i * BLOCK_Q + u * lanes - j * BLOCK_K, s, NEGATIVE)
            old = top[row, at]
            new = jnp.maximum(old, jnp.max(s, axis=0, keepdims=True))
            p = jnp.exp2(s - new)
            shrink = jnp.exp2(old - new)
            top[row, at] = new
            total[row, at] = total[row, at] * shrink + jnp.sum(p, axis=0, keepdims=True)
            acc[c, :, at] = acc[c, :, at] * shrink + nn(v, p.astype(bf16))

    run_tiles(chunks * chunk, count, tiles, prepare, process)
    for c in range(chunks):
        t = total[c : c + 1, :]
        o = acc[c] / t
        wide_ref[c] = o
        o_ref[c] = o.astype(bf16)
        lse_ref[0, c : c + 1, :] = top[c : c + 1, :] + jnp.log2(t)


def attend_back_body(count, tiles, x_ref, g_ref, wide_ref, lse_ref, segment_ref, scale_ref, dx_ref, part_ref, key_rows, query_cols, value_rows, dq, dk, dv, delta, scores, grads, *, chunks, chunk):
    nk = chunks * chunk // BLOCK_K
    per_q, per_k = chunk // BLOCK_Q, chunk // BLOCK_K
    lanes = BLOCK_Q // PARTS
    for c in range(chunks):
        hot = lax.broadcasted_iota(jnp.int32, (IDS, chunk), 0) == segment_ref[0, c : c + 1, :]
        keys = jnp.concatenate([x_ref[c, 0, 1], jnp.where(hot, 1.0, 0.0).astype(bf16)], axis=0)
        key_rows[pl.ds(c * chunk, chunk), :] = keys.T
        query_cols[c] = jnp.concatenate([x_ref[c, 0, 0], jnp.where(hot, 0.0, NEGATIVE).astype(bf16)], axis=0)
        value_rows[pl.ds(c * chunk, chunk), :] = x_ref[c, 0, 2].T
        delta[c : c + 1, :] = jnp.sum(g_ref[c].astype(f32) * wide_ref[c], axis=0, keepdims=True)
        for ref in (dq, dk, dv):
            ref[c] = jnp.zeros((HD, chunk), f32)
    key_iota = lax.broadcasted_iota(jnp.int32, (BLOCK_K, lanes), 0)
    query_iota = lax.broadcasted_iota(jnp.int32, (BLOCK_K, lanes), 1)

    def prepare(tile, slot):
        c, off = place(tile // nk, per_q, BLOCK_Q)
        rows = pl.ds(pl.multiple_of((tile % nk) * BLOCK_K, BLOCK_K), BLOCK_K)
        k, v = key_rows[rows, :], value_rows[rows, :]
        for u in range(PARTS):
            at = pl.ds(off + u * lanes, lanes)
            scores[slot, :, u * lanes : (u + 1) * lanes] = nn(k, query_cols[c, :, at])
            grads[slot, :, u * lanes : (u + 1) * lanes] = nn(v, g_ref[c, :, at])

    def process(tile, slot, masked):
        i, j = tile // nk, tile % nk
        c, off = place(i, per_q, BLOCK_Q)
        kc, koff = place(j, per_k, BLOCK_K)
        kat = pl.ds(koff, BLOCK_K)
        kt = x_ref[kc, 0, 1, :, kat]
        for u in range(PARTS):
            at = pl.ds(off + u * lanes, lanes)
            row = pl.ds(c, 1)
            s = scores[slot, :, u * lanes : (u + 1) * lanes] * LOG2E
            if masked:
                s = jnp.where(key_iota - query_iota <= i * BLOCK_Q + u * lanes - j * BLOCK_K, s, NEGATIVE)
            p = jnp.exp2(s - lse_ref[0, row, at])
            low = (p * (grads[slot, :, u * lanes : (u + 1) * lanes] - delta[row, at])).astype(bf16)
            q, g = x_ref[c, 0, 0, :, at], g_ref[c, :, at]
            dv[kc, :, kat] += nt(g, p.astype(bf16))
            dk[kc, :, kat] += nt(q, low)
            dq[c, :, at] += nn(kt, low)

    run_tiles(chunks * chunk, count, tiles, prepare, process)
    part = jnp.zeros((HD, 128), f32)
    for c in range(chunks):
        grad = dq[c]
        dx_ref[c, 0] = (grad * scale_ref[:, 0:1]).astype(bf16)
        dx_ref[c, 1] = dk[c].astype(bf16)
        dx_ref[c, 2] = dv[c].astype(bf16)
        term = grad * x_ref[c, 0, 0].astype(f32)
        for u in range(chunk // 128):
            part = part + term[:, u * 128 : (u + 1) * 128]
    part_ref[...] = part


def kernel_cost(length, matmuls):
    pairs = length * 2048
    return pl.CostEstimate(
        flops=matmuls * 512 * pairs, bytes_accessed=length * 2048, transcendentals=pairs
    )


def attend(tables, x, segments, p):
    chunks, _, _, _, chunk = x.shape
    flat = lambda g, *_: (0, 0, 0)
    return pl.pallas_call(
        functools.partial(attend_body, chunks=chunks, chunk=chunk),
        grid_spec=pltpu.PrefetchScalarGridSpec(
            num_scalar_prefetch=2,
            grid=(1,),
            in_specs=[
                pl.BlockSpec((chunks, 1, 3, HD, chunk), lambda g, *_: (0, p, 0, 0, 0)),
                pl.BlockSpec((1, chunks, chunk), flat),
            ],
            out_specs=[
                pl.BlockSpec((chunks, HD, chunk), flat),
                pl.BlockSpec((chunks, HD, chunk), flat),
                pl.BlockSpec((1, chunks, chunk), flat),
            ],
            scratch_shapes=[
                pltpu.VMEM((chunks * chunk, WIDE), bf16),
                pltpu.VMEM((chunks, WIDE, chunk), bf16),
                pltpu.VMEM((chunks, HD, chunk), f32),
                pltpu.VMEM((chunks, chunk), f32),
                pltpu.VMEM((chunks, chunk), f32),
                pltpu.VMEM((2, BLOCK_K, BLOCK_Q), f32),
            ],
        ),
        out_shape=[
            jax.ShapeDtypeStruct((chunks, HD, chunk), bf16),
            jax.ShapeDtypeStruct((chunks, HD, chunk), f32),
            jax.ShapeDtypeStruct((1, chunks, chunk), f32),
        ],
        compiler_params=pltpu.CompilerParams(vmem_limit_bytes=VMEM_BYTES),
        cost_estimate=kernel_cost(chunks * chunk, 2),
        name="attend",
    )(*tables, x, segments)


def attend_back(tables, x, grad, wide, lse, segments, scale, p):
    chunks, _, _, _, chunk = x.shape
    flat = lambda g, *_: (0, 0, 0)
    return pl.pallas_call(
        functools.partial(attend_back_body, chunks=chunks, chunk=chunk),
        grid_spec=pltpu.PrefetchScalarGridSpec(
            num_scalar_prefetch=2,
            grid=(1,),
            in_specs=[
                pl.BlockSpec((chunks, 1, 3, HD, chunk), lambda g, *_: (0, p, 0, 0, 0)),
                pl.BlockSpec((chunks, HD, chunk), flat),
                pl.BlockSpec((chunks, HD, chunk), flat),
                pl.BlockSpec((1, chunks, chunk), flat),
                pl.BlockSpec((1, chunks, chunk), flat),
                pl.BlockSpec((HD, 128), lambda g, *_: (0, 0)),
            ],
            out_specs=[
                pl.BlockSpec((chunks, 3, HD, chunk), lambda g, *_: (0, 0, 0, 0)),
                pl.BlockSpec((HD, 128), lambda g, *_: (0, 0)),
            ],
            scratch_shapes=[
                pltpu.VMEM((chunks * chunk, WIDE), bf16),
                pltpu.VMEM((chunks, WIDE, chunk), bf16),
                pltpu.VMEM((chunks * chunk, HD), bf16),
                pltpu.VMEM((chunks, HD, chunk), f32),
                pltpu.VMEM((chunks, HD, chunk), f32),
                pltpu.VMEM((chunks, HD, chunk), f32),
                pltpu.VMEM((chunks, chunk), f32),
                pltpu.VMEM((2, BLOCK_K, BLOCK_Q), f32),
                pltpu.VMEM((2, BLOCK_K, BLOCK_Q), f32),
            ],
        ),
        out_shape=[
            jax.ShapeDtypeStruct((chunks, 3, HD, chunk), bf16),
            jax.ShapeDtypeStruct((HD, 128), f32),
        ],
        compiler_params=pltpu.CompilerParams(vmem_limit_bytes=VMEM_BYTES),
        cost_estimate=kernel_cost(chunks * chunk, 5),
        name="attend_back",
    )(*tables, x, grad, wide, lse, segments, scale)


def project_body(slots_ref, w_ref, scale_ref, *refs, places):
    n = len(places)
    pieces, (out_ref, done_ref, buffers, results, in_sems, out_sems) = refs[:n], refs[-6:]
    done_ref[...] = jnp.zeros(done_ref.shape, f32)

    def fetch(i):
        return pltpu.make_async_copy(pieces[i], buffers.at[i], in_sems.at[i])

    def store(i):
        first, rows = places[i], results.shape[2]
        return pltpu.make_async_copy(
            results.at[i], out_ref.at[slots_ref[i], :, pl.ds(first, rows)], out_sems.at[i]
        )

    for i in range(n):
        fetch(i).start()
    for i in range(n):
        fetch(i).wait()
        results[i] = (nt(w_ref[...], buffers[i]) * scale_ref[...]).astype(bf16)
        store(i).start()
    for i in range(n):
        store(i).wait()


def project_into(heads, after, shape, slots, places, w, scale, pieces):
    features, width = w.shape
    n, rows = len(pieces), pieces[0].shape[0]
    kept = [] if heads is None else [heads]
    tail = [] if after is None else [after]
    whole = pl.BlockSpec(memory_space=pltpu.VMEM)
    anywhere = pl.BlockSpec(memory_space=pl.ANY)
    return pl.pallas_call(
        functools.partial(project_body, places=places),
        in_specs=[pl.BlockSpec(memory_space=pltpu.SMEM), whole, whole] + [anywhere] * (n + len(kept) + len(tail)),
        out_specs=[anywhere, whole],
        out_shape=[jax.ShapeDtypeStruct(shape, bf16), jax.ShapeDtypeStruct((8, 128), f32)],
        scratch_shapes=[
            pltpu.VMEM((n, rows, width), bf16),
            pltpu.VMEM((n, features, rows), bf16),
            pltpu.SemaphoreType.DMA((n,)),
            pltpu.SemaphoreType.DMA((n,)),
        ],
        input_output_aliases={3 + n: 0} if kept else {},
        compiler_params=pltpu.CompilerParams(vmem_limit_bytes=VMEM_BYTES),
        cost_estimate=pl.CostEstimate(
            flops=2 * n * features * width * rows, bytes_accessed=4 * n * width * rows, transcendentals=0
        ),
        name="project",
    )(slots, w, scale, *pieces, *kept, *tail)


def weight_grad_body(me_ref, *refs, spots):
    n = len(spots)
    pieces, (w_ref, dx, out_ref, gain_ref, buffers, acc, sems) = refs[:n], refs[n:]
    rows, width = buffers.shape[1:]

    def copy(i):
        return pltpu.make_async_copy(pieces[i], buffers.at[i], sems.at[i])

    for i in range(n):
        copy(i).start()
    for i, (distance, first) in enumerate(spots):
        part_dx = dx[me_ref[0] ^ distance, :, :, first : first + rows]
        part_dx = part_dx.reshape(part_dx.shape[0] * part_dx.shape[1], rows)
        copy(i).wait()
        for lane in range(0, width, 256):
            part = nn(part_dx, buffers[i, :, lane : lane + 256])
            acc[:, lane : lane + 256] = part + acc[:, lane : lane + 256] if i else part
    total = acc[...]
    out_ref[...] = total.astype(bf16)
    gain_ref[...] = jnp.sum(total * w_ref[...].astype(f32), axis=0, keepdims=True)


def weight_grad(me, pieces, spots, w, dx):
    features, width = w.shape
    whole = pl.BlockSpec(memory_space=pltpu.VMEM)
    return pl.pallas_call(
        functools.partial(weight_grad_body, spots=spots),
        in_specs=[pl.BlockSpec(memory_space=pltpu.SMEM)]
        + [pl.BlockSpec(memory_space=pl.ANY)] * len(pieces)
        + [whole] * 2,
        out_specs=[whole, whole],
        out_shape=[
            jax.ShapeDtypeStruct((features, width), bf16),
            jax.ShapeDtypeStruct((1, width), f32),
        ],
        scratch_shapes=[
            pltpu.VMEM((len(pieces),) + pieces[0].shape, bf16),
            pltpu.VMEM((features, width), f32),
            pltpu.SemaphoreType.DMA((len(pieces),)),
        ],
        compiler_params=pltpu.CompilerParams(vmem_limit_bytes=VMEM_BYTES),
        cost_estimate=pl.CostEstimate(flops=1, bytes_accessed=1, transcendentals=0),
        name="weight_grad",
    )(me, *pieces, w, dx)


def back_one_body(back_ref, w_ref, out_ref):
    out_ref[...] = nn(w_ref[...], back_ref[...]).T


def finish_body(back_ref, w_ref, other_ref, tokens_ref, gain_ref, hidden_ref, out_ref):
    grad_normed = other_ref[...] + nn(w_ref[...], back_ref[...]).T
    inputs = tokens_ref[...].astype(f32)
    inverse = inverse_rms(inputs)
    out_ref[...] = (
        hidden_ref[...] + norm_back(grad_normed, inputs * inverse, inverse, gain_ref[...])
    ).astype(bf16)


def input_grad(back, w, p, others):
    features, rows = back.shape
    width = w.shape[0]
    block = math.gcd(rows, 256)
    by_tokens = pl.BlockSpec((block, width), lambda t: (t, 0))
    specs = [by_tokens, by_tokens, pl.BlockSpec((1, width), lambda t: (0, 0)), by_tokens] if others else []
    return pl.pallas_call(
        finish_body if others else back_one_body,
        grid=(rows // block,),
        in_specs=[
            pl.BlockSpec((features, block), lambda t: (0, t)),
            pl.BlockSpec((width, features), lambda t: (0, p)),
        ]
        + specs,
        out_specs=by_tokens,
        out_shape=jax.ShapeDtypeStruct((rows, width), bf16 if others else f32),
        compiler_params=pltpu.CompilerParams(vmem_limit_bytes=VMEM_BYTES),
        cost_estimate=pl.CostEstimate(
            flops=2 * features * width * rows if others else 1,
            bytes_accessed=16 * width * rows if others else 1,
            transcendentals=0,
        ),
        name="input_grad",
    )(back, w, *others)


def head_grad_body(low_ref, w_ref, out_ref):
    out_ref[...] = nn(low_ref[...], w_ref[0]).T.astype(bf16)


def head_grad(low, whole, p, features):
    rows, width = low.shape
    block = math.gcd(rows, 256)
    return pl.pallas_call(
        head_grad_body,
        grid=(rows // block,),
        in_specs=[
            pl.BlockSpec((block, width), lambda t: (t, 0)),
            pl.BlockSpec((1, width, features), lambda t: (0, 0, p)),
        ],
        out_specs=pl.BlockSpec((features, block), lambda t: (0, t)),
        out_shape=jax.ShapeDtypeStruct((features, rows), bf16),
        compiler_params=pltpu.CompilerParams(vmem_limit_bytes=VMEM_BYTES),
        cost_estimate=pl.CostEstimate(flops=1, bytes_accessed=1, transcendentals=0),
        name="head_grad",
    )(low, whole)


def grad_act_body(top_ref, w_ref, out_ref):
    out_ref[...] = nn(top_ref[...], w_ref[0])


def grad_act_of(top, whole):
    rows, width = top.shape
    units = whole.shape[2]
    block = math.gcd(rows, 256)
    return pl.pallas_call(
        grad_act_body,
        grid=(rows // block,),
        in_specs=[
            pl.BlockSpec((block, width), lambda t: (t, 0)),
            pl.BlockSpec((1, width, units), lambda t: (2, 0, 0)),
        ],
        out_specs=pl.BlockSpec((block, units), lambda t: (t, 0)),
        out_shape=jax.ShapeDtypeStruct((rows, units), f32),
        compiler_params=pltpu.CompilerParams(vmem_limit_bytes=VMEM_BYTES),
        cost_estimate=pl.CostEstimate(flops=1, bytes_accessed=1, transcendentals=0),
        name="grad_act",
    )(top, whole)


def first_out_body(mixed_ref, w_ref, tokens_ref, out_ref):
    out_ref[...] = tokens_ref[...].astype(f32) + nn(w_ref[0], mixed_ref[...]).T


def first_out(mixed, whole, tokens):
    features, rows = mixed.shape
    width = tokens.shape[1]
    block = math.gcd(rows, 256)
    by_tokens = pl.BlockSpec((block, width), lambda t: (t, 0))
    return pl.pallas_call(
        first_out_body,
        grid=(rows // block,),
        in_specs=[
            pl.BlockSpec((features, block), lambda t: (0, t)),
            pl.BlockSpec((1, width, features), lambda t: (0, 0, 0)),
            by_tokens,
        ],
        out_specs=by_tokens,
        out_shape=jax.ShapeDtypeStruct((rows, width), f32),
        compiler_params=pltpu.CompilerParams(vmem_limit_bytes=VMEM_BYTES),
        cost_estimate=pl.CostEstimate(flops=1, bytes_accessed=1, transcendentals=0),
        name="first_out",
    )(mixed, whole, tokens)


def outputs_body(act_ref, w_ref, hidden_ref, bias_ref, out_ref):
    out_ref[...] = (hidden_ref[...] + (nt(act_ref[...], w_ref[0]) + bias_ref[...])).astype(bf16)


def down_outputs(act, whole, hidden, bias):
    rows, width = hidden.shape
    block = math.gcd(rows, 256)
    by_tokens = lambda n: pl.BlockSpec((block, n), lambda t: (t, 0))
    return pl.pallas_call(
        outputs_body,
        grid=(rows // block,),
        in_specs=[
            by_tokens(act.shape[1]),
            pl.BlockSpec((1, width, act.shape[1]), lambda t: (2, 0, 0)),
            by_tokens(width),
            pl.BlockSpec((1, width), lambda t: (0, 0)),
        ],
        out_specs=by_tokens(width),
        out_shape=jax.ShapeDtypeStruct((rows, width), bf16),
        compiler_params=pltpu.CompilerParams(vmem_limit_bytes=VMEM_BYTES),
        cost_estimate=pl.CostEstimate(flops=1, bytes_accessed=1, transcendentals=0),
        name="outputs",
    )(act, whole, hidden, bias[None])


def tile_list(segments):
    length = segments.shape[0]
    n_q, n_k = length // BLOCK_Q, length // BLOCK_K
    first = jnp.sum(segments[None, :] < segments[::BLOCK_Q][:, None], axis=1, dtype=jnp.int32)[:, None]
    q_block = jnp.arange(n_q, dtype=jnp.int32)[:, None]
    k_last = jnp.arange(n_k, dtype=jnp.int32)[None, :] * BLOCK_K + BLOCK_K - 1
    below = ((k_last < q_block * BLOCK_Q) & (k_last >= first)).reshape(-1)
    pair = jnp.arange(n_q * n_k, dtype=jnp.int32)
    rank = jnp.sum(jnp.where((pair[None, :] <= pair[:, None]) & below[None, :], 1, 0), axis=1) - 1
    count = rank[-1] + 1
    spot = jnp.arange(n_q * n_k + 2, dtype=jnp.int32)
    chosen = jnp.where(below, rank, -1)[None, :] == spot[:, None]
    tiles = jnp.sum(jnp.where(chosen, pair[None, :], 0), axis=1)
    tiles = jnp.where(spot == count, n_k - 1, tiles)
    return (count + count % 2).reshape(1), tiles


def in_rows(grad):
    return with_layout_constraint(grad.astype(bf16), Layout((0, 1)))


def inverse_rms(values):
    return lax.rsqrt(jnp.mean(values * values, axis=-1, keepdims=True) + EPSILON)


def norm_back(grad_norm, unit, inverse, gain):
    grad_unit = grad_norm * gain
    return inverse * (grad_unit - unit * jnp.mean(grad_unit * unit, axis=-1, keepdims=True))


def per_device(
    tokens,
    segments,
    gain_attn,
    query_scale,
    w_qkv,
    w_out,
    gain_mlp,
    w_up,
    b_up,
    w_down,
    b_down,
    cotangent,
):
    n_dp, n_ctx, n_tensor = (lax.axis_size(a) for a in ("dp", "ctx", "tensor"))
    ctx_rank, tensor_rank = lax.axis_index("ctx"), lax.axis_index("tensor")
    rows, sequences, width = tokens.shape
    shard, columns = w_qkv.shape[1:]
    local_heads = columns // HD
    group = n_ctx * n_tensor
    length = rows * group
    data = ("dp", "ctx")
    everyone = ("dp", "ctx", "tensor")
    split = local_heads % n_ctx == 0
    ctx_parts = n_ctx if split else 1
    own = local_heads // ctx_parts
    owners = ("ctx", "tensor") if split else ("tensor",)
    n_owners = ctx_parts * n_tensor
    head_width = own * 3 * HD

    inputs = tokens[:, 0].astype(f32)
    inverse_one = inverse_rms(inputs)
    unit_one = inputs * inverse_one
    normed_one = (unit_one * gain_attn).astype(bf16)

    def other_side(x):
        if n_tensor != 2:
            return lax.all_gather(x, "tensor", axis=0)
        return lax.ppermute(x, "tensor", [(0, 1), (1, 0)])

    def in_order(x, other):
        if n_tensor != 2:
            return other
        first = tensor_rank == 0
        return jnp.stack([jnp.where(first, x, other), jnp.where(first, other, x)])

    def scatter_pair(x):
        if n_tensor != 2:
            return lax.psum_scatter(x, "tensor", scatter_dimension=0, tiled=False).astype(f32)
        keep = jnp.where(tensor_rank == 0, x[0], x[1])
        send = jnp.where(tensor_rank == 0, x[1], x[0])
        return keep.astype(f32) + lax.ppermute(send, "tensor", [(0, 1), (1, 0)]).astype(f32)

    def by_distance(x, rank):
        count = x.shape[0]
        bit = 1
        while bit < count:
            y = x.reshape((count // (2 * bit), 2, bit) + x.shape[1:])
            y = jnp.where((rank & bit) > 0, jnp.flip(y, 1), y)
            x = y.reshape(x.shape)
            bit *= 2
        return x

    def exchange(x, axis, rank):
        count = x.shape[0]
        x = by_distance(x, rank)
        got = [x[0]] + [
            lax.ppermute(x[k], axis, [(i, i ^ k) for i in range(count)]) for k in range(1, count)
        ]
        return by_distance(jnp.stack(got), rank)

    qkv_rows = w_qkv.reshape(3, shard, ctx_parts, own, HD)
    for_owner = qkv_rows.transpose(2, 1, 3, 0, 4).reshape(ctx_parts, shard, head_width)
    if split:
        for_owner = exchange(for_owner, "ctx", ctx_rank)
    others = [other_side(w) for w in (w_qkv, w_out, w_up, w_down)]
    halves = [normed_one[: rows // 2], normed_one[rows // 2 :]]
    halves, for_owner, others = lax.optimization_barrier((halves, for_owner, others))
    pairs = [in_order(w, other) for w, other in zip((w_qkv, w_out, w_up, w_down), others, strict=True)]
    if split:
        owner_w = lax.all_gather(for_owner, "dp", axis=0).reshape(width, head_width)
    else:
        owner_w = lax.all_gather(for_owner[0], data, axis=0).reshape(width, head_width)

    tiles = tile_list(segments[0])
    qkv_cols = pairs[0].reshape(n_tensor, 3, shard, ctx_parts, own, HD).transpose(0, 2, 4, 3, 1, 5)
    out_cols = pairs[1].reshape(n_tensor, ctx_parts, own, HD, shard).transpose(0, 4, 2, 1, 3)

    def interleave(x, inner):
        x = x.reshape(n_tensor, shard, own * ctx_parts, inner)
        return x.transpose(1, 2, 0, 3).reshape(shard, -1)

    def side_by_side(x):
        return x.transpose(1, 0, 2).reshape(shard, -1)

    full_rows = jnp.stack(
        [
            interleave(out_cols, HD),
            side_by_side(pairs[2]),
            side_by_side(jnp.swapaxes(pairs[3], 1, 2)),
        ]
    )
    qkv_rows_full = interleave(qkv_cols, 3 * HD)
    scaling = LOG_TWO_E / math.sqrt(HD) * jax.nn.softplus(query_scale)
    scale_rows = jnp.tile(
        jnp.concatenate([scaling, jnp.ones((2 * HD,), f32)]), own
    )[:, None]

    w_rows = owner_w.T
    if group == 8 and n_tensor == 2:
        me = ctx_rank * n_tensor + tensor_rank
        spots, pieces = [], []

        def swap(x, bit):
            return lax.ppermute(x, ("ctx", "tensor"), [(i, i ^ bit) for i in range(group)])

        def add(heads_x, after, parts):
            spots.extend((distance, first) for distance, first, _ in parts)
            pieces.extend(piece for _, _, piece in parts)
            slots = jnp.stack([me ^ distance for distance, _, _ in parts])
            places = [first for _, first, _ in parts]
            shape = (group, head_width, rows)
            return project_into(heads_x, after, shape, slots, places, w_rows, scale_rows, [piece for _, _, piece in parts])

        def with_core(distance, low, high):
            return [
                (distance ^ bit, first, swap(piece, bit) if bit else piece)
                for bit in (0, 2)
                for first, piece in ((0, low), (rows // 2, high))
            ]

        own_parts = with_core(0, *halves)
        heads_x, _ = add(None, None, own_parts[:2])
        heads_x, done = add(heads_x, None, own_parts[2:])
        over_x, over_y = [swap(halves[0], 1)], [swap(halves[1], 4)]
        over_x.append(swap(halves[1], 1))
        over_y.append(swap(halves[0], 4))
        corner = [swap(over_x[0], 4), swap(over_y[0], 1)]
        over_x, over_y, full_rows, qkv_rows_full, tiles, done = lax.optimization_barrier(
            (over_x, over_y, full_rows, qkv_rows_full, tiles, done)
        )
        heads_x, done = add(heads_x, done, with_core(1, *over_x))
        heads_x, done = add(heads_x, done, with_core(4, over_y[1], over_y[0]))
        corner, done = lax.optimization_barrier((corner, done))
        heads_x, _ = add(heads_x, done, with_core(5, *corner))
    else:
        spots = None
        normed_all = lax.all_gather(normed_one, ("ctx", "tensor"), axis=0)
        heads_x = (nt(w_rows, normed_all.reshape(length, width)) * scale_rows).astype(bf16)
        heads_x = heads_x.reshape(head_width, group, rows).transpose(1, 0, 2)
    whole = lax.all_gather(full_rows, data, axis=1, tiled=True)
    out_t, up_all, down_t = whole[0], whole[1], whole[2]
    qkv_all = lax.all_gather(qkv_rows_full, data, axis=0, tiled=True)

    chunk = max(rows, BLOCK_Q, BLOCK_K)
    merge = chunk // rows
    chunks = length // chunk

    def to_chunks(x):
        if merge == 1:
            return x
        x = jnp.moveaxis(x.reshape((chunks, merge) + x.shape[1:]), 1, -2)
        return x.reshape(x.shape[:-2] + (chunk,))

    def from_chunks(x):
        if merge == 1:
            return x
        x = jnp.moveaxis(x.reshape(x.shape[:-1] + (merge, rows)), -2, 1)
        return x.reshape((group,) + x.shape[2:])

    def to_tokens(x):
        x = from_chunks(x)
        if not split:
            x = lax.dynamic_slice_in_dim(x, ctx_rank * n_tensor, n_tensor, 0)
        return lax.all_to_all(x, owners, 0, 0)

    def to_heads(x):
        x = lax.all_to_all(x, owners, 0, 0)
        if not split:
            x = lax.all_gather(x, "ctx", axis=0, tiled=True)
        return to_chunks(x)

    heads_x = to_chunks(heads_x)
    heads_x = heads_x.reshape(chunks, own, 3, HD, chunk)
    seg_chunks = segments.reshape(1, chunks, chunk)

    part = n_owners * HD

    mixed, wides, lses = [], [], []
    for p in range(own):
        o, wide, lse = attend(tiles, heads_x, seg_chunks, p)
        wides.append(wide)
        lses.append(lse)
        if p == own - 1:
            o, top_low = lax.optimization_barrier((o, cotangent[:, 0]))
        mixed.append(to_tokens(o).reshape(part, rows))
    grad_act = grad_act_of(top_low, whole)
    hidden = inputs
    if own > 1:
        hidden = first_out(mixed[0], whole, tokens[:, 0])
    mixed[-1], grad_act, hidden = lax.optimization_barrier((mixed[-1], grad_act, hidden))

    for p in range(1 if own > 1 else 0, own):
        hidden = hidden + dot(mixed[p], out_t[:, p * part : (p + 1) * part], (0,), (1,))
    inverse_two = inverse_rms(hidden)
    unit_two = hidden * inverse_two
    normed_two = (unit_two * gain_mlp).astype(bf16)
    pre_act = nn(normed_two, up_all) + b_up
    sigma = jax.nn.sigmoid(pre_act)
    activation = (pre_act * sigma).astype(bf16)
    grad_top = top_low.astype(f32)
    grad_pre = (grad_act * (sigma * (1 + pre_act * (1 - sigma)))).astype(bf16)
    grad_normed_two = nt(grad_pre, up_all)
    grad_hidden = grad_top + norm_back(grad_normed_two, unit_two, inverse_two, gain_mlp)
    grad_hidden_low = grad_hidden.astype(bf16)
    grad_heads = [nt(out_t[:, :part].T, grad_hidden_low).astype(bf16)]
    grad_heads += [head_grad(grad_hidden_low, whole, p, part) for p in range(1, own)]
    grad_heads = [g.reshape(n_owners, HD, rows) for g in grad_heads]
    grad_heads[0], low, act, normed = lax.optimization_barrier(
        (grad_heads[0], grad_hidden_low, activation, normed_two)
    )
    outputs = down_outputs(act, whole, hidden, b_down)
    grad_heads[-1], outputs = lax.optimization_barrier((grad_heads[-1], outputs))
    grad_heads = [to_heads(g) for g in grad_heads]
    grad_out_t = [dot(low, m, (0,), (1,)) for m in mixed]
    grad_up = dot(normed, grad_pre, (0,), (0,))
    grad_down_t = dot(top_low, act, (0,), (0,))
    stacked = jnp.concatenate([in_rows(g) for g in (*grad_out_t, grad_up, grad_down_t)], axis=1)
    stacked, qkv_all = lax.optimization_barrier((stacked, qkv_all))
    reduced = lax.psum_scatter(stacked, data, scatter_dimension=0, tiled=True)
    reduced = [reduced[:, n * width : (n + 1) * width] for n in range(3)]
    gain_two = jnp.sum(grad_normed_two * unit_two, axis=0)
    bias_up = jnp.sum(grad_pre.astype(f32), axis=0)
    bias_down = jnp.sum(grad_top, axis=0)
    scale_tile = jnp.broadcast_to(scaling[:, None], (HD, 128))
    scale_sum = jnp.zeros((HD,), f32)
    gain_part = jnp.zeros((width,), f32)
    dxs, backs, wgrads, travelled = [], [], [], []
    for p in range(own):
        dx, part_sum = attend_back(
            tiles, heads_x, grad_heads[p], wides[p], lses[p], seg_chunks, scale_tile, p
        )
        if p:
            dx, backs[-1] = lax.optimization_barrier((dx, backs[-1]))
        scale_sum = scale_sum + jnp.sum(part_sum, axis=1)
        backs.append(to_tokens(dx).reshape(3 * part, rows))
        dxs.append(dx)
    dxs = lax.optimization_barrier(dxs)
    for p, dx in enumerate(dxs):
        if p == own - 1:
            grad_normed_one = jnp.zeros((rows, width), f32)
            for n in range(own - 1):
                backs[n], wgrads[n] = lax.optimization_barrier((backs[n], wgrads[n]))
                grad_normed_one = grad_normed_one + input_grad(backs[n], qkv_all, n, ())
            dx, grad_normed_one = lax.optimization_barrier((dx, grad_normed_one))
        if spots is None:
            grad_w = lax.dot_general(
                to_chunks(jnp.swapaxes(normed_all, 1, 2)),
                dx.reshape(chunks, 3 * HD, chunk),
                (((0, 2), (0, 2)), ((), ())),
                preferred_element_type=f32,
            )
            weights_p = owner_w.reshape(width, own, 3 * HD)[:, p].astype(f32)
            gain_part = gain_part + jnp.sum(grad_w * weights_p, axis=1)
            wgrads.append(grad_w.astype(bf16))
        else:
            own_w = w_rows[p * 3 * HD : (p + 1) * 3 * HD]
            grad_w, gain_add = weight_grad(me.reshape(1), pieces, spots, own_w, dx)
            wgrads.append(grad_w.T)
            gain_part = gain_part + gain_add[0]
        if p == own - 1:
            split_out = reduced[0].reshape(shard, own, ctx_parts, n_tensor, HD).transpose(3, 0, 2, 1, 4)
            split_up, split_down = (
                reduced[n].reshape(shard, n_tensor, columns).transpose(1, 0, 2) for n in (1, 2)
            )
            halves_of = jnp.stack([split_out.reshape(n_tensor, shard, columns), split_up, split_down], axis=1)
            wgrads[-1], gain_part, backs[-1], halves_of, travelled = lax.optimization_barrier(
                (wgrads[-1], gain_part, backs[-1], halves_of, travelled)
            )
        rows_by = by_distance(wgrads[-1].reshape(n_dp, n_ctx * shard, 3 * HD), lax.axis_index("dp"))
        wgrads[-1] = rows_by[0]
        travelled.append(
            [lax.ppermute(rows_by[k], "dp", [(i, i ^ k) for i in range(n_dp)]) for k in range(1, n_dp)]
        )
    gain_one, scale_sum = gain_part / gain_attn, scale_sum / scaling
    if not split:
        once = (ctx_rank == 0).astype(f32)
        gain_one, scale_sum = gain_one * once, scale_sum * once

    def doubled(x, axis):
        count, bit = lax.axis_size(axis), 1
        while bit < count:
            x = x + lax.ppermute(x, axis, [(i, i ^ bit) for i in range(count)])
            bit *= 2
        return x

    sums = jnp.concatenate([gain_one, gain_two, bias_up, bias_down, scale_sum])
    small = all(n & (n - 1) == 0 and n <= 4 for n in (n_dp, n_ctx, n_tensor))
    if small:
        sums = doubled(sums, "dp")
    piece = jnp.concatenate(
        [sum((g.astype(f32) for g in far), w.astype(f32)).astype(bf16) for w, far in zip(wgrads, travelled, strict=True)],
        axis=1,
    )
    grad_inputs = input_grad(
        backs[-1], qkv_all, own - 1, (grad_normed_one, tokens[:, 0], gain_attn[None], grad_hidden)
    )
    mine = scatter_pair(halves_of)
    piece, sums, grad_inputs, mine = lax.optimization_barrier((piece, sums, grad_inputs, mine))
    out_grad, up_grad, down_grad = mine[0].T, mine[1], mine[2].T
    piece = piece.reshape(n_ctx, shard, head_width)
    if split:
        piece = exchange(piece, "ctx", ctx_rank)
    else:
        piece = lax.dynamic_slice_in_dim(piece, ctx_rank, 1, 0)
    if small:
        sums = doubled(sums, "ctx")
        sums, piece = lax.optimization_barrier((sums, piece))
        sums = doubled(sums, "tensor")
    else:
        sums = lax.psum(sums, everyone)
    qkv_grad = piece.reshape(ctx_parts, shard, own, 3, HD).transpose(3, 1, 0, 2, 4)
    qkv_grad = qkv_grad.reshape(w_qkv.shape).astype(f32)

    gain_one, gain_two, bias_up, bias_down = (sums[n * width : (n + 1) * width] for n in range(4))
    grad_query_scale = sums[4 * width :] * (LOG_TWO_E / math.sqrt(HD)) * jax.nn.sigmoid(query_scale)
    return (
        outputs[:, None],
        grad_inputs[:, None],
        qkv_grad,
        out_grad,
        up_grad,
        down_grad,
        gain_one,
        grad_query_scale,
        gain_two,
        bias_up,
        bias_down,
    )


def solution(mesh):
    placed = (
        P(("ctx", "tensor"), "dp", None),
        P("dp", None),
        P(),
        P(),
        P(None, ("dp", "ctx"), "tensor"),
        P("tensor", ("dp", "ctx")),
        P(),
        P(("dp", "ctx"), "tensor"),
        P(),
        P("tensor", ("dp", "ctx")),
        P(),
        P(("ctx", "tensor"), "dp", None),
    )
    return jax.shard_map(
        per_device,
        mesh=mesh,
        in_specs=placed,
        out_specs=(
            P(("ctx", "tensor"), "dp", None),
            P(("ctx", "tensor"), "dp", None),
            P(None, ("dp", "ctx"), "tensor"),
            P("tensor", ("dp", "ctx")),
            P(("dp", "ctx"), "tensor"),
            P("tensor", ("dp", "ctx")),
            P(),
            P(),
            P(),
            P(),
            P(),
        ),
        check_vma=False,
    )
```

```python
import functools
import math

import jax
import jax.numpy as jnp
from jax import lax
from jax.experimental import pallas as pl
from jax.experimental.layout import Layout, with_layout_constraint
from jax.experimental.pallas import tpu as pltpu
from jax.sharding import PartitionSpec as P

HD = 80
IDS = 32
BLOCK_Q = 512
BLOCK_K = 512
PARTS = 2
WIDE = HD + IDS
EPSILON = 1e-06
LOG_TWO_E = 1.442695041
LOG2E = 1.4426950408889634
NEGATIVE = -1e30
VMEM_BYTES = 60 << 20
bf16, f32 = jnp.bfloat16, jnp.float32


def dot(a, b, contract_a, contract_b):
    return lax.dot_general(
        a, b, ((contract_a, contract_b), ((), ())), preferred_element_type=f32
    )


def nn(a, b):
    return dot(a, b, (1,), (0,))


def nt(a, b):
    return dot(a, b, (1,), (1,))


def place(block, per, size):
    return block // per, pl.multiple_of((block % per) * size, size)


def run_tiles(length, count, tiles, prepare, process):
    n_q, n_k = length // BLOCK_Q, length // BLOCK_K

    def diagonal(t):
        t = jnp.minimum(t, n_q - 1)
        return t * n_k + t * BLOCK_Q // BLOCK_K

    def turns(number, tile, masked):
        prepare(tile(0), 0)

        def turn(t, _):
            prepare(tile(2 * t + 1), 1)
            process(tile(2 * t), 0, masked)
            prepare(tile(2 * t + 2), 0)
            process(tile(2 * t + 1), 1, masked)
            return 0

        lax.fori_loop(0, number, turn, 0)

    turns(n_q // 2, diagonal, True)
    turns(count[0] // 2, lambda t: tiles[t], False)


def attend_body(count, tiles, x_ref, segment_ref, o_ref, lse_ref, key_rows, query_cols, acc, top, total, scores, *, chunks, chunk):
    nk = chunks * chunk // BLOCK_K
    per_q, per_k = chunk // BLOCK_Q, chunk // BLOCK_K
    lanes = BLOCK_Q // PARTS
    for c in range(chunks):
        hot = lax.broadcasted_iota(jnp.int32, (IDS, chunk), 0) == segment_ref[0, c : c + 1, :]
        keys = jnp.concatenate([x_ref[c, 0, 1], jnp.where(hot, 1.0, 0.0).astype(bf16)], axis=0)
        key_rows[pl.ds(c * chunk, chunk), :] = keys.T
        query_cols[c] = jnp.concatenate([x_ref[c, 0, 0], jnp.where(hot, 0.0, NEGATIVE).astype(bf16)], axis=0)
        acc[c] = jnp.zeros((HD, chunk), f32)
    top[...] = jnp.full(top.shape, NEGATIVE, f32)
    total[...] = jnp.zeros(total.shape, f32)
    key_iota = lax.broadcasted_iota(jnp.int32, (BLOCK_K, lanes), 0)
    query_iota = lax.broadcasted_iota(jnp.int32, (BLOCK_K, lanes), 1)

    def prepare(tile, slot):
        c, off = place(tile // nk, per_q, BLOCK_Q)
        k = key_rows[pl.ds(pl.multiple_of((tile % nk) * BLOCK_K, BLOCK_K), BLOCK_K), :]
        for u in range(PARTS):
            scores[slot, :, u * lanes : (u + 1) * lanes] = nn(k, query_cols[c, :, pl.ds(off + u * lanes, lanes)]) * LOG2E

    def process(tile, slot, masked):
        i, j = tile // nk, tile % nk
        c, off = place(i, per_q, BLOCK_Q)
        ck_, koff = place(j, per_k, BLOCK_K)
        v = x_ref[ck_, 0, 2, :, pl.ds(koff, BLOCK_K)]
        for u in range(PARTS):
            at = pl.ds(off + u * lanes, lanes)
            row = pl.ds(c, 1)
            s = scores[slot, :, u * lanes : (u + 1) * lanes]
            if masked:
                s = jnp.where(key_iota - query_iota <= i * BLOCK_Q + u * lanes - j * BLOCK_K, s, NEGATIVE)
            old = top[row, at]
            new = jnp.maximum(old, jnp.max(s, axis=0, keepdims=True))
            p = jnp.exp2(s - new)
            shrink = jnp.exp2(old - new)
            top[row, at] = new
            total[row, at] = total[row, at] * shrink + jnp.sum(p, axis=0, keepdims=True)
            acc[c, :, at] = acc[c, :, at] * shrink + nn(v, p.astype(bf16))

    run_tiles(chunks * chunk, count, tiles, prepare, process)
    for c in range(chunks):
        t = total[c : c + 1, :]
        o = acc[c] / t
        o_ref[c] = o.astype(bf16)
        lse_ref[0, c : c + 1, :] = top[c : c + 1, :] + jnp.log2(t)


def attend_back_body(count, tiles, x_ref, g_ref, mixed_ref, lse_ref, segment_ref, scale_ref, dx_ref, part_ref, key_rows, query_cols, value_rows, dq, dk, dv, delta, scores, grads, *, chunks, chunk):
    nk = chunks * chunk // BLOCK_K
    per_q, per_k = chunk // BLOCK_Q, chunk // BLOCK_K
    lanes = BLOCK_Q // PARTS
    for c in range(chunks):
        hot = lax.broadcasted_iota(jnp.int32, (IDS, chunk), 0) == segment_ref[0, c : c + 1, :]
        keys = jnp.concatenate([x_ref[c, 0, 1], jnp.where(hot, 1.0, 0.0).astype(bf16)], axis=0)
        key_rows[pl.ds(c * chunk, chunk), :] = keys.T
        query_cols[c] = jnp.concatenate([x_ref[c, 0, 0], jnp.where(hot, 0.0, NEGATIVE).astype(bf16)], axis=0)
        value_rows[pl.ds(c * chunk, chunk), :] = x_ref[c, 0, 2].T
        delta[c : c + 1, :] = jnp.sum(g_ref[c].astype(f32) * mixed_ref[c].astype(f32), axis=0, keepdims=True)
        for ref in (dq, dk, dv):
            ref[c] = jnp.zeros((HD, chunk), f32)
    key_iota = lax.broadcasted_iota(jnp.int32, (BLOCK_K, lanes), 0)
    query_iota = lax.broadcasted_iota(jnp.int32, (BLOCK_K, lanes), 1)

    def prepare(tile, slot):
        c, off = place(tile // nk, per_q, BLOCK_Q)
        rows = pl.ds(pl.multiple_of((tile % nk) * BLOCK_K, BLOCK_K), BLOCK_K)
        k, v = key_rows[rows, :], value_rows[rows, :]
        for u in range(PARTS):
            at = pl.ds(off + u * lanes, lanes)
            scores[slot, :, u * lanes : (u + 1) * lanes] = nn(k, query_cols[c, :, at])
            grads[slot, :, u * lanes : (u + 1) * lanes] = nn(v, g_ref[c, :, at])

    def process(tile, slot, masked):
        i, j = tile // nk, tile % nk
        c, off = place(i, per_q, BLOCK_Q)
        kc, koff = place(j, per_k, BLOCK_K)
        kat = pl.ds(koff, BLOCK_K)
        kt = x_ref[kc, 0, 1, :, kat]
        for u in range(PARTS):
            at = pl.ds(off + u * lanes, lanes)
            row = pl.ds(c, 1)
            s = scores[slot, :, u * lanes : (u + 1) * lanes] * LOG2E
            if masked:
                s = jnp.where(key_iota - query_iota <= i * BLOCK_Q + u * lanes - j * BLOCK_K, s, NEGATIVE)
            p = jnp.exp2(s - lse_ref[0, row, at])
            low = (p * (grads[slot, :, u * lanes : (u + 1) * lanes] - delta[row, at])).astype(bf16)
            q, g = x_ref[c, 0, 0, :, at], g_ref[c, :, at]
            dv[kc, :, kat] += nt(g, p.astype(bf16))
            dk[kc, :, kat] += nt(q, low)
            dq[c, :, at] += nn(kt, low)

    run_tiles(chunks * chunk, count, tiles, prepare, process)
    part = jnp.zeros((HD, 128), f32)
    for c in range(chunks):
        grad = dq[c]
        dx_ref[c, 0] = (grad * scale_ref[:, 0:1]).astype(bf16)
        dx_ref[c, 1] = dk[c].astype(bf16)
        dx_ref[c, 2] = dv[c].astype(bf16)
        term = grad * x_ref[c, 0, 0].astype(f32)
        for u in range(chunk // 128):
            part = part + term[:, u * 128 : (u + 1) * 128]
    part_ref[...] = part


def kernel_cost(length, matmuls):
    pairs = length * 2048
    return pl.CostEstimate(
        flops=matmuls * 512 * pairs, bytes_accessed=length * 2048, transcendentals=pairs
    )


def attend(tables, x, segments, p):
    chunks, _, _, _, chunk = x.shape
    flat = lambda g, *_: (0, 0, 0)
    return pl.pallas_call(
        functools.partial(attend_body, chunks=chunks, chunk=chunk),
        grid_spec=pltpu.PrefetchScalarGridSpec(
            num_scalar_prefetch=2,
            grid=(1,),
            in_specs=[
                pl.BlockSpec((chunks, 1, 3, HD, chunk), lambda g, *_: (0, p, 0, 0, 0)),
                pl.BlockSpec((1, chunks, chunk), flat),
            ],
            out_specs=[
                pl.BlockSpec((chunks, HD, chunk), flat),
                pl.BlockSpec((1, chunks, chunk), flat),
            ],
            scratch_shapes=[
                pltpu.VMEM((chunks * chunk, WIDE), bf16),
                pltpu.VMEM((chunks, WIDE, chunk), bf16),
                pltpu.VMEM((chunks, HD, chunk), f32),
                pltpu.VMEM((chunks, chunk), f32),
                pltpu.VMEM((chunks, chunk), f32),
                pltpu.VMEM((2, BLOCK_K, BLOCK_Q), f32),
            ],
        ),
        out_shape=[
            jax.ShapeDtypeStruct((chunks, HD, chunk), bf16),
            jax.ShapeDtypeStruct((1, chunks, chunk), f32),
        ],
        compiler_params=pltpu.CompilerParams(vmem_limit_bytes=VMEM_BYTES),
        cost_estimate=kernel_cost(chunks * chunk, 2),
        name="attend",
    )(*tables, x, segments)


def attend_back(tables, x, grad, mixed, lse, segments, scale, p):
    chunks, _, _, _, chunk = x.shape
    flat = lambda g, *_: (0, 0, 0)
    return pl.pallas_call(
        functools.partial(attend_back_body, chunks=chunks, chunk=chunk),
        grid_spec=pltpu.PrefetchScalarGridSpec(
            num_scalar_prefetch=2,
            grid=(1,),
            in_specs=[
                pl.BlockSpec((chunks, 1, 3, HD, chunk), lambda g, *_: (0, p, 0, 0, 0)),
                pl.BlockSpec((chunks, HD, chunk), flat),
                pl.BlockSpec((chunks, HD, chunk), flat),
                pl.BlockSpec((1, chunks, chunk), flat),
                pl.BlockSpec((1, chunks, chunk), flat),
                pl.BlockSpec((HD, 128), lambda g, *_: (0, 0)),
            ],
            out_specs=[
                pl.BlockSpec((chunks, 3, HD, chunk), lambda g, *_: (0, 0, 0, 0)),
                pl.BlockSpec((HD, 128), lambda g, *_: (0, 0)),
            ],
            scratch_shapes=[
                pltpu.VMEM((chunks * chunk, WIDE), bf16),
                pltpu.VMEM((chunks, WIDE, chunk), bf16),
                pltpu.VMEM((chunks * chunk, HD), bf16),
                pltpu.VMEM((chunks, HD, chunk), f32),
                pltpu.VMEM((chunks, HD, chunk), f32),
                pltpu.VMEM((chunks, HD, chunk), f32),
                pltpu.VMEM((chunks, chunk), f32),
                pltpu.VMEM((2, BLOCK_K, BLOCK_Q), f32),
                pltpu.VMEM((2, BLOCK_K, BLOCK_Q), f32),
            ],
        ),
        out_shape=[
            jax.ShapeDtypeStruct((chunks, 3, HD, chunk), bf16),
            jax.ShapeDtypeStruct((HD, 128), f32),
        ],
        compiler_params=pltpu.CompilerParams(vmem_limit_bytes=VMEM_BYTES),
        cost_estimate=kernel_cost(chunks * chunk, 5),
        name="attend_back",
    )(*tables, x, grad, mixed, lse, segments, scale)


def project_body(slots_ref, w_ref, scale_ref, *refs, places):
    n = len(places)
    pieces, (out_ref, done_ref, buffers, results, in_sems, out_sems) = refs[:n], refs[-6:]
    done_ref[...] = jnp.zeros(done_ref.shape, f32)

    def fetch(i):
        return pltpu.make_async_copy(pieces[i], buffers.at[i], in_sems.at[i])

    def store(i):
        first, rows = places[i], results.shape[2]
        return pltpu.make_async_copy(
            results.at[i], out_ref.at[slots_ref[i], :, pl.ds(first, rows)], out_sems.at[i]
        )

    for i in range(n):
        fetch(i).start()
    for i in range(n):
        fetch(i).wait()
        results[i] = (nt(w_ref[...], buffers[i]) * scale_ref[...]).astype(bf16)
        store(i).start()
    for i in range(n):
        store(i).wait()


def project_into(heads, after, shape, slots, places, w, scale, pieces):
    features, width = w.shape
    n, rows = len(pieces), pieces[0].shape[0]
    kept = [] if heads is None else [heads]
    tail = [] if after is None else [after]
    whole = pl.BlockSpec(memory_space=pltpu.VMEM)
    anywhere = pl.BlockSpec(memory_space=pl.ANY)
    return pl.pallas_call(
        functools.partial(project_body, places=places),
        in_specs=[pl.BlockSpec(memory_space=pltpu.SMEM), whole, whole] + [anywhere] * (n + len(kept) + len(tail)),
        out_specs=[anywhere, whole],
        out_shape=[jax.ShapeDtypeStruct(shape, bf16), jax.ShapeDtypeStruct((8, 128), f32)],
        scratch_shapes=[
            pltpu.VMEM((n, rows, width), bf16),
            pltpu.VMEM((n, features, rows), bf16),
            pltpu.SemaphoreType.DMA((n,)),
            pltpu.SemaphoreType.DMA((n,)),
        ],
        input_output_aliases={3 + n: 0} if kept else {},
        compiler_params=pltpu.CompilerParams(vmem_limit_bytes=VMEM_BYTES),
        cost_estimate=pl.CostEstimate(
            flops=2 * n * features * width * rows, bytes_accessed=4 * n * width * rows, transcendentals=0
        ),
        name="project",
    )(slots, w, scale, *pieces, *kept, *tail)


def weight_grad_body(me_ref, *refs, spots):
    n = len(spots)
    pieces, (w_ref, dx, out_ref, gain_ref, buffers, acc, sems) = refs[:n], refs[n:]
    rows, width = buffers.shape[1:]

    def copy(i):
        return pltpu.make_async_copy(pieces[i], buffers.at[i], sems.at[i])

    for i in range(n):
        copy(i).start()
    for i, (distance, first) in enumerate(spots):
        part_dx = dx[me_ref[0] ^ distance, :, :, first : first + rows]
        part_dx = part_dx.reshape(part_dx.shape[0] * part_dx.shape[1], rows)
        copy(i).wait()
        for lane in range(0, width, 256):
            part = nn(part_dx, buffers[i, :, lane : lane + 256])
            acc[:, lane : lane + 256] = part + acc[:, lane : lane + 256] if i else part
    total = acc[...]
    out_ref[...] = total.astype(bf16)
    gain_ref[...] = jnp.sum(total * w_ref[...].astype(f32), axis=0, keepdims=True)


def weight_grad(me, pieces, spots, w, dx):
    features, width = w.shape
    whole = pl.BlockSpec(memory_space=pltpu.VMEM)
    return pl.pallas_call(
        functools.partial(weight_grad_body, spots=spots),
        in_specs=[pl.BlockSpec(memory_space=pltpu.SMEM)]
        + [pl.BlockSpec(memory_space=pl.ANY)] * len(pieces)
        + [whole] * 2,
        out_specs=[whole, whole],
        out_shape=[
            jax.ShapeDtypeStruct((features, width), bf16),
            jax.ShapeDtypeStruct((1, width), f32),
        ],
        scratch_shapes=[
            pltpu.VMEM((len(pieces),) + pieces[0].shape, bf16),
            pltpu.VMEM((features, width), f32),
            pltpu.SemaphoreType.DMA((len(pieces),)),
        ],
        compiler_params=pltpu.CompilerParams(vmem_limit_bytes=VMEM_BYTES),
        cost_estimate=pl.CostEstimate(flops=1, bytes_accessed=1, transcendentals=0),
        name="weight_grad",
    )(me, *pieces, w, dx)


def back_one_body(back_ref, w_ref, out_ref):
    out_ref[...] = nn(w_ref[...], back_ref[...]).T


def finish_body(back_ref, w_ref, other_ref, tokens_ref, gain_ref, hidden_ref, out_ref):
    grad_normed = other_ref[...] + nn(w_ref[...], back_ref[...]).T
    inputs = tokens_ref[...].astype(f32)
    inverse = inverse_rms(inputs)
    out_ref[...] = (
        hidden_ref[...] + norm_back(grad_normed, inputs * inverse, inverse, gain_ref[...])
    ).astype(bf16)


def input_grad(back, w, p, others):
    features, rows = back.shape
    width = w.shape[0]
    block = math.gcd(rows, 256)
    by_tokens = pl.BlockSpec((block, width), lambda t: (t, 0))
    specs = [by_tokens, by_tokens, pl.BlockSpec((1, width), lambda t: (0, 0)), by_tokens] if others else []
    return pl.pallas_call(
        finish_body if others else back_one_body,
        grid=(rows // block,),
        in_specs=[
            pl.BlockSpec((features, block), lambda t: (0, t)),
            pl.BlockSpec((width, features), lambda t: (0, p)),
        ]
        + specs,
        out_specs=by_tokens,
        out_shape=jax.ShapeDtypeStruct((rows, width), bf16 if others else f32),
        compiler_params=pltpu.CompilerParams(vmem_limit_bytes=VMEM_BYTES),
        cost_estimate=pl.CostEstimate(
            flops=2 * features * width * rows if others else 1,
            bytes_accessed=16 * width * rows if others else 1,
            transcendentals=0,
        ),
        name="input_grad",
    )(back, w, *others)


def head_grad_body(low_ref, w_ref, out_ref):
    out_ref[...] = nn(low_ref[...], w_ref[0]).T.astype(bf16)


def head_grad(low, whole, p, features):
    rows, width = low.shape
    block = math.gcd(rows, 256)
    return pl.pallas_call(
        head_grad_body,
        grid=(rows // block,),
        in_specs=[
            pl.BlockSpec((block, width), lambda t: (t, 0)),
            pl.BlockSpec((1, width, features), lambda t: (0, 0, p)),
        ],
        out_specs=pl.BlockSpec((features, block), lambda t: (0, t)),
        out_shape=jax.ShapeDtypeStruct((features, rows), bf16),
        compiler_params=pltpu.CompilerParams(vmem_limit_bytes=VMEM_BYTES),
        cost_estimate=pl.CostEstimate(flops=1, bytes_accessed=1, transcendentals=0),
        name="head_grad",
    )(low, whole)


def grad_act_body(top_ref, w_ref, out_ref):
    out_ref[...] = nn(top_ref[...], w_ref[0])


def grad_act_of(top, whole):
    rows, width = top.shape
    units = whole.shape[2]
    block = math.gcd(rows, 256)
    return pl.pallas_call(
        grad_act_body,
        grid=(rows // block,),
        in_specs=[
            pl.BlockSpec((block, width), lambda t: (t, 0)),
            pl.BlockSpec((1, width, units), lambda t: (2, 0, 0)),
        ],
        out_specs=pl.BlockSpec((block, units), lambda t: (t, 0)),
        out_shape=jax.ShapeDtypeStruct((rows, units), f32),
        compiler_params=pltpu.CompilerParams(vmem_limit_bytes=VMEM_BYTES),
        cost_estimate=pl.CostEstimate(flops=1, bytes_accessed=1, transcendentals=0),
        name="grad_act",
    )(top, whole)


def first_out_body(mixed_ref, w_ref, tokens_ref, out_ref):
    out_ref[...] = tokens_ref[...].astype(f32) + nn(w_ref[0], mixed_ref[...]).T


def first_out(mixed, whole, tokens):
    features, rows = mixed.shape
    width = tokens.shape[1]
    block = math.gcd(rows, 256)
    by_tokens = pl.BlockSpec((block, width), lambda t: (t, 0))
    return pl.pallas_call(
        first_out_body,
        grid=(rows // block,),
        in_specs=[
            pl.BlockSpec((features, block), lambda t: (0, t)),
            pl.BlockSpec((1, width, features), lambda t: (0, 0, 0)),
            by_tokens,
        ],
        out_specs=by_tokens,
        out_shape=jax.ShapeDtypeStruct((rows, width), f32),
        compiler_params=pltpu.CompilerParams(vmem_limit_bytes=VMEM_BYTES),
        cost_estimate=pl.CostEstimate(flops=1, bytes_accessed=1, transcendentals=0),
        name="first_out",
    )(mixed, whole, tokens)


def outputs_body(act_ref, w_ref, hidden_ref, bias_ref, out_ref):
    out_ref[...] = (hidden_ref[...] + (nt(act_ref[...], w_ref[0]) + bias_ref[...])).astype(bf16)


def down_outputs(act, whole, hidden, bias):
    rows, width = hidden.shape
    block = math.gcd(rows, 256)
    by_tokens = lambda n: pl.BlockSpec((block, n), lambda t: (t, 0))
    return pl.pallas_call(
        outputs_body,
        grid=(rows // block,),
        in_specs=[
            by_tokens(act.shape[1]),
            pl.BlockSpec((1, width, act.shape[1]), lambda t: (2, 0, 0)),
            by_tokens(width),
            pl.BlockSpec((1, width), lambda t: (0, 0)),
        ],
        out_specs=by_tokens(width),
        out_shape=jax.ShapeDtypeStruct((rows, width), bf16),
        compiler_params=pltpu.CompilerParams(vmem_limit_bytes=VMEM_BYTES),
        cost_estimate=pl.CostEstimate(flops=1, bytes_accessed=1, transcendentals=0),
        name="outputs",
    )(act, whole, hidden, bias[None])


def tile_list(segments):
    length = segments.shape[0]
    n_q, n_k = length // BLOCK_Q, length // BLOCK_K
    first = jnp.sum(segments[None, :] < segments[::BLOCK_Q][:, None], axis=1, dtype=jnp.int32)[:, None]
    q_block = jnp.arange(n_q, dtype=jnp.int32)[:, None]
    k_last = jnp.arange(n_k, dtype=jnp.int32)[None, :] * BLOCK_K + BLOCK_K - 1
    below = ((k_last < q_block * BLOCK_Q) & (k_last >= first)).reshape(-1)
    pair = jnp.arange(n_q * n_k, dtype=jnp.int32)
    rank = jnp.sum(jnp.where((pair[None, :] <= pair[:, None]) & below[None, :], 1, 0), axis=1) - 1
    count = rank[-1] + 1
    spot = jnp.arange(n_q * n_k + 2, dtype=jnp.int32)
    chosen = jnp.where(below, rank, -1)[None, :] == spot[:, None]
    tiles = jnp.sum(jnp.where(chosen, pair[None, :], 0), axis=1)
    tiles = jnp.where(spot == count, n_k - 1, tiles)
    return (count + count % 2).reshape(1), tiles


def in_rows(grad):
    return with_layout_constraint(grad.astype(bf16), Layout((0, 1)))


def inverse_rms(values):
    return lax.rsqrt(jnp.mean(values * values, axis=-1, keepdims=True) + EPSILON)


def norm_back(grad_norm, unit, inverse, gain):
    grad_unit = grad_norm * gain
    return inverse * (grad_unit - unit * jnp.mean(grad_unit * unit, axis=-1, keepdims=True))


def per_device(
    tokens,
    segments,
    gain_attn,
    query_scale,
    w_qkv,
    w_out,
    gain_mlp,
    w_up,
    b_up,
    w_down,
    b_down,
    cotangent,
):
    n_dp, n_ctx, n_tensor = (lax.axis_size(a) for a in ("dp", "ctx", "tensor"))
    ctx_rank, tensor_rank = lax.axis_index("ctx"), lax.axis_index("tensor")
    rows, sequences, width = tokens.shape
    shard, columns = w_qkv.shape[1:]
    local_heads = columns // HD
    group = n_ctx * n_tensor
    length = rows * group
    data = ("dp", "ctx")
    everyone = ("dp", "ctx", "tensor")
    split = local_heads % n_ctx == 0
    ctx_parts = n_ctx if split else 1
    own = local_heads // ctx_parts
    owners = ("ctx", "tensor") if split else ("tensor",)
    n_owners = ctx_parts * n_tensor
    head_width = own * 3 * HD

    inputs = tokens[:, 0].astype(f32)
    inverse_one = inverse_rms(inputs)
    unit_one = inputs * inverse_one
    normed_one = (unit_one * gain_attn).astype(bf16)

    def other_side(x):
        if n_tensor != 2:
            return lax.all_gather(x, "tensor", axis=0)
        return lax.ppermute(x, "tensor", [(0, 1), (1, 0)])

    def in_order(x, other):
        if n_tensor != 2:
            return other
        first = tensor_rank == 0
        return jnp.stack([jnp.where(first, x, other), jnp.where(first, other, x)])

    def scatter_pair(x):
        if n_tensor != 2:
            return lax.psum_scatter(x, "tensor", scatter_dimension=0, tiled=False).astype(f32)
        keep = jnp.where(tensor_rank == 0, x[0], x[1])
        send = jnp.where(tensor_rank == 0, x[1], x[0])
        return keep.astype(f32) + lax.ppermute(send, "tensor", [(0, 1), (1, 0)]).astype(f32)

    def by_distance(x, rank):
        count = x.shape[0]
        bit = 1
        while bit < count:
            y = x.reshape((count // (2 * bit), 2, bit) + x.shape[1:])
            y = jnp.where((rank & bit) > 0, jnp.flip(y, 1), y)
            x = y.reshape(x.shape)
            bit *= 2
        return x

    def exchange(x, axis, rank):
        count = x.shape[0]
        x = by_distance(x, rank)
        got = [x[0]] + [
            lax.ppermute(x[k], axis, [(i, i ^ k) for i in range(count)]) for k in range(1, count)
        ]
        return by_distance(jnp.stack(got), rank)

    qkv_rows = w_qkv.reshape(3, shard, ctx_parts, own, HD)
    for_owner = qkv_rows.transpose(2, 1, 3, 0, 4).reshape(ctx_parts, shard, head_width)
    if split:
        for_owner = exchange(for_owner, "ctx", ctx_rank)
    others = [other_side(w) for w in (w_qkv, w_out, w_up, w_down)]
    halves = [normed_one[: rows // 2], normed_one[rows // 2 :]]
    halves, for_owner, others = lax.optimization_barrier((halves, for_owner, others))
    pairs = [in_order(w, other) for w, other in zip((w_qkv, w_out, w_up, w_down), others, strict=True)]
    if split:
        owner_w = lax.all_gather(for_owner, "dp", axis=0).reshape(width, head_width)
    else:
        owner_w = lax.all_gather(for_owner[0], data, axis=0).reshape(width, head_width)

    tiles = tile_list(segments[0])
    qkv_cols = pairs[0].reshape(n_tensor, 3, shard, ctx_parts, own, HD).transpose(0, 2, 4, 3, 1, 5)
    out_cols = pairs[1].reshape(n_tensor, ctx_parts, own, HD, shard).transpose(0, 4, 2, 1, 3)

    def interleave(x, inner):
        x = x.reshape(n_tensor, shard, own * ctx_parts, inner)
        return x.transpose(1, 2, 0, 3).reshape(shard, -1)

    def side_by_side(x):
        return x.transpose(1, 0, 2).reshape(shard, -1)

    full_rows = jnp.stack(
        [
            interleave(out_cols, HD),
            side_by_side(pairs[2]),
            side_by_side(jnp.swapaxes(pairs[3], 1, 2)),
        ]
    )
    qkv_rows_full = interleave(qkv_cols, 3 * HD)
    scaling = LOG_TWO_E / math.sqrt(HD) * jax.nn.softplus(query_scale)
    scale_rows = jnp.tile(
        jnp.concatenate([scaling, jnp.ones((2 * HD,), f32)]), own
    )[:, None]

    w_rows = owner_w.T
    if group == 8 and n_tensor == 2:
        me = ctx_rank * n_tensor + tensor_rank
        spots, pieces = [], []

        def swap(x, bit):
            return lax.ppermute(x, ("ctx", "tensor"), [(i, i ^ bit) for i in range(group)])

        def add(heads_x, after, parts):
            spots.extend((distance, first) for distance, first, _ in parts)
            pieces.extend(piece for _, _, piece in parts)
            slots = jnp.stack([me ^ distance for distance, _, _ in parts])
            places = [first for _, first, _ in parts]
            shape = (group, head_width, rows)
            return project_into(heads_x, after, shape, slots, places, w_rows, scale_rows, [piece for _, _, piece in parts])

        def with_core(distance, low, high):
            return [
                (distance ^ bit, first, swap(piece, bit) if bit else piece)
                for bit in (0, 2)
                for first, piece in ((0, low), (rows // 2, high))
            ]

        own_parts = with_core(0, *halves)
        heads_x, _ = add(None, None, own_parts[:2])
        heads_x, done = add(heads_x, None, own_parts[2:])
        over_x, over_y = [swap(halves[0], 1)], [swap(halves[1], 4)]
        over_x.append(swap(halves[1], 1))
        over_y.append(swap(halves[0], 4))
        corner = [swap(over_x[0], 4), swap(over_y[0], 1)]
        over_x, over_y, full_rows, qkv_rows_full, tiles, done = lax.optimization_barrier(
            (over_x, over_y, full_rows, qkv_rows_full, tiles, done)
        )
        heads_x, done = add(heads_x, done, with_core(1, *over_x))
        heads_x, done = add(heads_x, done, with_core(4, over_y[1], over_y[0]))
        corner, done = lax.optimization_barrier((corner, done))
        heads_x, _ = add(heads_x, done, with_core(5, *corner))
    else:
        spots = None
        normed_all = lax.all_gather(normed_one, ("ctx", "tensor"), axis=0)
        heads_x = (nt(w_rows, normed_all.reshape(length, width)) * scale_rows).astype(bf16)
        heads_x = heads_x.reshape(head_width, group, rows).transpose(1, 0, 2)
    whole = lax.all_gather(full_rows, data, axis=1, tiled=True)
    out_t, up_all, down_t = whole[0], whole[1], whole[2]
    qkv_all = lax.all_gather(qkv_rows_full, data, axis=0, tiled=True)

    chunk = max(rows, BLOCK_Q, BLOCK_K)
    merge = chunk // rows
    chunks = length // chunk

    def to_chunks(x):
        if merge == 1:
            return x
        x = jnp.moveaxis(x.reshape((chunks, merge) + x.shape[1:]), 1, -2)
        return x.reshape(x.shape[:-2] + (chunk,))

    def from_chunks(x):
        if merge == 1:
            return x
        x = jnp.moveaxis(x.reshape(x.shape[:-1] + (merge, rows)), -2, 1)
        return x.reshape((group,) + x.shape[2:])

    def to_tokens(x):
        x = from_chunks(x)
        if not split:
            x = lax.dynamic_slice_in_dim(x, ctx_rank * n_tensor, n_tensor, 0)
        return lax.all_to_all(x, owners, 0, 0)

    def to_heads(x):
        x = lax.all_to_all(x, owners, 0, 0)
        if not split:
            x = lax.all_gather(x, "ctx", axis=0, tiled=True)
        return to_chunks(x)

    heads_x = to_chunks(heads_x)
    heads_x = heads_x.reshape(chunks, own, 3, HD, chunk)
    seg_chunks = segments.reshape(1, chunks, chunk)

    part = n_owners * HD

    mixed, head_outs, lses = [], [], []
    for p in range(own):
        o, lse = attend(tiles, heads_x, seg_chunks, p)
        head_outs.append(o)
        lses.append(lse)
        if p == own - 1:
            o, top_low = lax.optimization_barrier((o, cotangent[:, 0]))
        mixed.append(to_tokens(o).reshape(part, rows))
    grad_act = grad_act_of(top_low, whole)
    hidden = inputs
    if own > 1:
        hidden = first_out(mixed[0], whole, tokens[:, 0])
    mixed[-1], grad_act, hidden = lax.optimization_barrier((mixed[-1], grad_act, hidden))

    for p in range(1 if own > 1 else 0, own):
        hidden = hidden + dot(mixed[p], out_t[:, p * part : (p + 1) * part], (0,), (1,))
    inverse_two = inverse_rms(hidden)
    unit_two = hidden * inverse_two
    normed_two = (unit_two * gain_mlp).astype(bf16)
    pre_act = nn(normed_two, up_all) + b_up
    sigma = jax.nn.sigmoid(pre_act)
    activation = (pre_act * sigma).astype(bf16)
    grad_top = top_low.astype(f32)
    grad_pre = (grad_act * (sigma * (1 + pre_act * (1 - sigma)))).astype(bf16)
    grad_normed_two = nt(grad_pre, up_all)
    grad_hidden = grad_top + norm_back(grad_normed_two, unit_two, inverse_two, gain_mlp)
    grad_hidden_low = grad_hidden.astype(bf16)
    grad_heads = [nt(out_t[:, :part].T, grad_hidden_low).astype(bf16)]
    grad_heads += [head_grad(grad_hidden_low, whole, p, part) for p in range(1, own)]
    grad_heads = [g.reshape(n_owners, HD, rows) for g in grad_heads]
    grad_heads[0], low, act, normed = lax.optimization_barrier(
        (grad_heads[0], grad_hidden_low, activation, normed_two)
    )
    outputs = down_outputs(act, whole, hidden, b_down)
    grad_heads[-1], outputs = lax.optimization_barrier((grad_heads[-1], outputs))
    grad_heads = [to_heads(g) for g in grad_heads]
    grad_out_t = [dot(low, m, (0,), (1,)) for m in mixed]
    grad_up = dot(normed, grad_pre, (0,), (0,))
    grad_down_t = dot(top_low, act, (0,), (0,))
    stacked = jnp.concatenate([in_rows(g) for g in (*grad_out_t, grad_up, grad_down_t)], axis=1)
    stacked, qkv_all = lax.optimization_barrier((stacked, qkv_all))
    reduced = lax.psum_scatter(stacked, data, scatter_dimension=0, tiled=True)
    reduced = [reduced[:, n * width : (n + 1) * width] for n in range(3)]
    gain_two = jnp.sum(grad_normed_two * unit_two, axis=0)
    bias_up = jnp.sum(grad_pre.astype(f32), axis=0)
    bias_down = jnp.sum(grad_top, axis=0)
    scale_tile = jnp.broadcast_to(scaling[:, None], (HD, 128))
    scale_sum = jnp.zeros((HD,), f32)
    gain_part = jnp.zeros((width,), f32)
    dxs, backs, wgrads, travelled = [], [], [], []
    for p in range(own):
        dx, part_sum = attend_back(
            tiles, heads_x, grad_heads[p], head_outs[p], lses[p], seg_chunks, scale_tile, p
        )
        if p:
            dx, backs[-1] = lax.optimization_barrier((dx, backs[-1]))
        scale_sum = scale_sum + jnp.sum(part_sum, axis=1)
        backs.append(to_tokens(dx).reshape(3 * part, rows))
        dxs.append(dx)
    dxs = lax.optimization_barrier(dxs)
    for p, dx in enumerate(dxs):
        if p == own - 1:
            grad_normed_one = jnp.zeros((rows, width), f32)
            for n in range(own - 1):
                backs[n], wgrads[n] = lax.optimization_barrier((backs[n], wgrads[n]))
                grad_normed_one = grad_normed_one + input_grad(backs[n], qkv_all, n, ())
            dx, grad_normed_one = lax.optimization_barrier((dx, grad_normed_one))
        if spots is None:
            grad_w = lax.dot_general(
                to_chunks(jnp.swapaxes(normed_all, 1, 2)),
                dx.reshape(chunks, 3 * HD, chunk),
                (((0, 2), (0, 2)), ((), ())),
                preferred_element_type=f32,
            )
            weights_p = owner_w.reshape(width, own, 3 * HD)[:, p].astype(f32)
            gain_part = gain_part + jnp.sum(grad_w * weights_p, axis=1)
            wgrads.append(grad_w.astype(bf16))
        else:
            own_w = w_rows[p * 3 * HD : (p + 1) * 3 * HD]
            grad_w, gain_add = weight_grad(me.reshape(1), pieces, spots, own_w, dx)
            wgrads.append(grad_w.T)
            gain_part = gain_part + gain_add[0]
        if p == own - 1:
            split_out = reduced[0].reshape(shard, own, ctx_parts, n_tensor, HD).transpose(3, 0, 2, 1, 4)
            split_up, split_down = (
                reduced[n].reshape(shard, n_tensor, columns).transpose(1, 0, 2) for n in (1, 2)
            )
            halves_of = jnp.stack([split_out.reshape(n_tensor, shard, columns), split_up, split_down], axis=1)
            wgrads[-1], gain_part, backs[-1], halves_of, travelled = lax.optimization_barrier(
                (wgrads[-1], gain_part, backs[-1], halves_of, travelled)
            )
        rows_by = by_distance(wgrads[-1].reshape(n_dp, n_ctx * shard, 3 * HD), lax.axis_index("dp"))
        wgrads[-1] = rows_by[0]
        travelled.append(
            [lax.ppermute(rows_by[k], "dp", [(i, i ^ k) for i in range(n_dp)]) for k in range(1, n_dp)]
        )
    gain_one, scale_sum = gain_part / gain_attn, scale_sum / scaling
    if not split:
        once = (ctx_rank == 0).astype(f32)
        gain_one, scale_sum = gain_one * once, scale_sum * once

    def doubled(x, axis):
        count, bit = lax.axis_size(axis), 1
        while bit < count:
            x = x + lax.ppermute(x, axis, [(i, i ^ bit) for i in range(count)])
            bit *= 2
        return x

    sums = jnp.concatenate([gain_one, gain_two, bias_up, bias_down, scale_sum])
    small = all(n & (n - 1) == 0 and n <= 4 for n in (n_dp, n_ctx, n_tensor))
    if small:
        sums = doubled(sums, "dp")
    piece = jnp.concatenate(
        [sum((g.astype(f32) for g in far), w.astype(f32)).astype(bf16) for w, far in zip(wgrads, travelled, strict=True)],
        axis=1,
    )
    grad_inputs = input_grad(
        backs[-1], qkv_all, own - 1, (grad_normed_one, tokens[:, 0], gain_attn[None], grad_hidden)
    )
    mine = scatter_pair(halves_of)
    piece, sums, grad_inputs, mine = lax.optimization_barrier((piece, sums, grad_inputs, mine))
    out_grad, up_grad, down_grad = mine[0].T, mine[1], mine[2].T
    piece = piece.reshape(n_ctx, shard, head_width)
    if split:
        piece = exchange(piece, "ctx", ctx_rank)
    else:
        piece = lax.dynamic_slice_in_dim(piece, ctx_rank, 1, 0)
    if small:
        sums = doubled(sums, "ctx")
        sums, piece = lax.optimization_barrier((sums, piece))
        sums = doubled(sums, "tensor")
    else:
        sums = lax.psum(sums, everyone)
    qkv_grad = piece.reshape(ctx_parts, shard, own, 3, HD).transpose(3, 1, 0, 2, 4)
    qkv_grad = qkv_grad.reshape(w_qkv.shape).astype(f32)

    gain_one, gain_two, bias_up, bias_down = (sums[n * width : (n + 1) * width] for n in range(4))
    grad_query_scale = sums[4 * width :] * (LOG_TWO_E / math.sqrt(HD)) * jax.nn.sigmoid(query_scale)
    return (
        outputs[:, None],
        grad_inputs[:, None],
        qkv_grad,
        out_grad,
        up_grad,
        down_grad,
        gain_one,
        grad_query_scale,
        gain_two,
        bias_up,
        bias_down,
    )


def solution(mesh):
    placed = (
        P(("ctx", "tensor"), "dp", None),
        P("dp", None),
        P(),
        P(),
        P(None, ("dp", "ctx"), "tensor"),
        P("tensor", ("dp", "ctx")),
        P(),
        P(("dp", "ctx"), "tensor"),
        P(),
        P("tensor", ("dp", "ctx")),
        P(),
        P(("ctx", "tensor"), "dp", None),
    )
    return jax.shard_map(
        per_device,
        mesh=mesh,
        in_specs=placed,
        out_specs=(
            P(("ctx", "tensor"), "dp", None),
            P(("ctx", "tensor"), "dp", None),
            P(None, ("dp", "ctx"), "tensor"),
            P("tensor", ("dp", "ctx")),
            P(("dp", "ctx"), "tensor"),
            P("tensor", ("dp", "ctx")),
            P(),
            P(),
            P(),
            P(),
            P(),
        ),
        check_vma=False,
    )
```
